32 devices in a mesh: dp: 8 (over z, y), rep: 4 (over x, core).
Axes of the slice: x: 2, y: 2, z: 4, core: 2. Of those that a mesh axis runs over, the one named last changes fastest.
Arguments:
- packet_bytes: int32 [4096, 256], P(('dp', 'rep')), may hold values from 0 to 255
- owner_index: int32 [4096], P(('dp', 'rep')), may hold values from 0 to 7, as said below
- session_id: int32 [4096], P(('dp', 'rep')), may hold values from 0 to 15
- class_label: int32 [512], P(('dp', 'rep')), may hold values from 0 to 127
- byte_table: bfloat16 [256, 64], replicated, may hold values from -6 to 6
- w_conv: bfloat16 [512, 512], replicated, may hold values from -0.25 to 0.25
- norm_gain: bfloat16 [512], replicated, may hold values from 0.099609375 to 1.8984375
- w_project: bfloat16 [512, 1536], replicated, may hold values from -7 to 7
- w_out: bfloat16 [512, 512], replicated, may hold values from -0.25 to 0.25
- w_head: bfloat16 [512, 128], replicated, may hold values from -4 to 4
Outputs:
- logits: float32 [512, 128], P(('dp', 'rep'))
- grad_table: float32 [256, 64], replicated
- grad_conv: float32 [512, 512], replicated
- grad_gain: float32 [512], replicated
- grad_project: float32 [512, 1536], replicated
- grad_out: float32 [512, 512], replicated
- grad_head: float32 [512, 128], replicated
The draws below stay inside these ranges and needn't reach their ends.
Inputs may be any that keep to these rules, and one draw needn't show every extreme that they name: `owner_index`: of one device's packets at most 32 name any one owner; in each group along dp one owner is named by exactly 32 packets of every device of the group.
All inputs are finite; a program needn't handle non-finite values.
Results may differ from the reference program's by a relative error of at most 0.01.
Values may be sent and summed in bfloat16 or wider, within the bound.
No kernel may reach another device: no remote copies, remote signals or barrier semaphores. Data moves between devices by JAX's collectives and lax.ppermute only.
A program may use at most 128 MiB of HBM per device.

```python
import jax
import jax.numpy as jnp
from jax import lax

PKT_DEV = 128
BYTES = 256
CHAN = 64
KERNEL = 8
D = 512
HEADS = 8
NCLS = 128
POS = 32
SESS = 16
PACKETS = 4096
SESS_ALL = 512
N_DP = 8
N_REP = 4


def draw_packet_bytes(key, part):
    devices = N_DP * N_REP
    order = jax.random.permutation(jax.random.fold_in(key, 4001), 256).astype(jnp.int32)
    device_ids = jnp.arange(devices, dtype=jnp.int32)
    common = order[device_ids % 256]
    drawn = jax.random.randint(jax.random.fold_in(key, 4002), (devices, PKT_DEV, BYTES), 0, 256)
    pick = jax.random.randint(jax.random.fold_in(key, 4003), (devices, PKT_DEV, BYTES), 0, 4)
    mixed = jnp.where(pick < 3, common[:, None, None], drawn)
    return mixed.reshape(devices * PKT_DEV, BYTES).astype(jnp.int32)


def draw_owner_index(key, part):
    capacity = 2 * PKT_DEV // N_DP
    slot_count = N_DP * capacity
    devices = N_DP * N_REP
    slot_ids = jnp.arange(slot_count, dtype=jnp.int32)
    slot_owner = slot_ids // capacity

    def one_device(index):
        group_key = jax.random.fold_in(key, 7001 + index % N_REP)
        biases = jax.random.randint(group_key, (N_DP,), 0, 3)
        hottest = jax.random.randint(jax.random.fold_in(group_key, 5), (), 0, N_DP)
        biases = jnp.where(jnp.arange(N_DP, dtype=jnp.int32) == hottest, 8, biases)
        own_key = jax.random.fold_in(key, index)
        noise = jax.random.randint(own_key, (slot_count,), 0, 2048)
        scores = (biases[slot_owner] * 1024 + noise) * 1024 + slot_ids
        picked = lax.top_k(scores, PKT_DEV)[1]
        owners = slot_owner[picked]
        order = jax.random.permutation(jax.random.fold_in(own_key, 3), PKT_DEV)
        return owners[order].astype(jnp.int32)
    return jax.vmap(one_device)(jnp.arange(devices, dtype=jnp.int32)).reshape(-1)


def draw_w_project(key, part):
    spread = D ** (-0.5)
    base = jnp.clip(jax.random.normal(key, (D, 3 * D), jnp.float32), -4.0, 4.0) * spread
    return base.astype(jnp.bfloat16)


def plant(entries, stream_key, least, top_value):
    longest = entries.shape.index(max(entries.shape))
    spots = []
    for shift in (0, 1):
        where = [jax.random.randint(jax.random.fold_in(stream_key, axis), (), 0, length) for axis, length in enumerate(entries.shape)]
        where[longest] = (where[longest] + shift) % entries.shape[longest]
        spots.append(tuple(where))
    return entries.at[spots[0]].set(least).at[spots[1]].set(top_value)


def centred(rng, dims, width, bound, held_as=jnp.bfloat16):
    result = jax.random.normal(rng, dims, jnp.float32) * width
    return jnp.minimum(jnp.maximum(result, -bound), bound).astype(held_as)


def setup_inputs(seed: int = 0) -> dict:
    splits = jax.random.split(jax.random.key(seed), 11)
    return {
        "packet_bytes": draw_packet_bytes(jax.random.fold_in(splits[10], 71), 0),
        "owner_index": draw_owner_index(jax.random.fold_in(splits[10], 71), 0),
        "session_id": plant(jax.random.randint(splits[2], (PACKETS,), 0, SESS), jax.random.fold_in(splits[2], 1), 0, SESS - 1).astype(jnp.int32),
        "class_label": plant(jax.random.randint(splits[3], (SESS_ALL,), 0, NCLS), jax.random.fold_in(splits[3], 1), 0, NCLS - 1).astype(jnp.int32),
        "byte_table": centred(splits[4], (256, CHAN), 1.0, 6.0),
        "w_conv": centred(splits[5], (KERNEL * CHAN, D), (KERNEL * CHAN) ** -0.5, 0.25),
        "norm_gain": jnp.clip(1.0 + 0.18 * jax.random.normal(splits[6], (D,), jnp.float32), 0.099609375, 1.8984375).astype(jnp.bfloat16),
        "w_project": draw_w_project(jax.random.fold_in(splits[10], 71), 0),
        "w_out": centred(splits[8], (D, D), D ** -0.5, 0.25),
        "w_head": centred(splits[9], (D, NCLS), 0.7, 4.0),
    }


NORM_EPS = 1e-06

def silu_slope(values_in):
    sigma = jax.nn.sigmoid(values_in)
    return sigma * (1.0 + values_in * (1.0 - sigma))

def windows_of(byte_codes, byte_table):
    feats = jnp.take(byte_table, byte_codes, axis=0)
    return feats.reshape(byte_codes.shape[0], BYTES // KERNEL, KERNEL * CHAN)

def session_layer(received, recv_session, labels_here, norm_gain, w_project, w_out, w_head):
    slot_count = received.shape[0]
    head_dim = D // HEADS
    score_scale = head_dim ** (-0.5)
    f32 = jnp.float32
    bf16 = jnp.bfloat16
    as_float = received.astype(f32)
    inverse = lax.rsqrt(lax.optimization_barrier(jnp.mean(as_float * as_float, axis=1, keepdims=True)) + NORM_EPS)
    gain_f = norm_gain.astype(f32)
    norm_in = (as_float * inverse * gain_f).astype(bf16)
    projected = jnp.dot(norm_in, w_project, preferred_element_type=f32).astype(bf16)
    projected = projected.reshape(slot_count, 3, HEADS, head_dim)
    queries = projected[:, 0].astype(f32)
    keys_all = projected[:, 1].astype(f32)
    values = projected[:, 2].astype(f32)
    same_session = recv_session[:, None] == recv_session[None, :]
    scores = jnp.einsum('qhd,khd->hqk', queries, keys_all) * score_scale
    scores = jnp.where(same_session[None], scores, -1e+30)
    row_max = lax.optimization_barrier(jnp.max(scores, axis=2, keepdims=True))
    shifted = jnp.exp(scores - row_max)
    mixing = shifted / lax.optimization_barrier(jnp.sum(shifted, axis=2, keepdims=True))
    mixing_b = mixing.astype(bf16)
    attended = jnp.einsum('hqk,khd->qhd', mixing_b.astype(f32), values).astype(bf16).reshape(slot_count, D)
    hidden = as_float + jnp.dot(attended, w_out, preferred_element_type=f32)
    member = (recv_session[None, :] == jnp.arange(SESS, dtype=jnp.int32)[:, None]).astype(f32)
    counts = jnp.maximum(lax.optimization_barrier(jnp.sum(member, axis=1, keepdims=True)), 1.0)
    pooled = jnp.dot(member, hidden, precision=lax.Precision.HIGHEST) / counts
    pooled_b = pooled.astype(bf16)
    logits = jnp.dot(pooled_b, w_head, preferred_element_type=f32)
    class_probs = jax.nn.softmax(logits, axis=1)
    target = (labels_here[:, None] == jnp.arange(NCLS, dtype=jnp.int32)[None, :]).astype(f32)
    dlogits = (class_probs - target) / SESS
    grad_head = jnp.dot(pooled_b.astype(f32).T, dlogits, precision=lax.Precision.HIGHEST)
    dpooled = jnp.dot(dlogits, w_head.astype(f32).T, precision=lax.Precision.HIGHEST)
    dhidden = jnp.dot(member.T, dpooled / counts, precision=lax.Precision.HIGHEST)
    dhidden_b = dhidden.astype(bf16)
    grad_out = jnp.dot(attended.T, dhidden_b, preferred_element_type=f32)
    dattended = jnp.dot(dhidden_b, w_out.T, preferred_element_type=f32).astype(bf16)
    dattended = dattended.reshape(slot_count, HEADS, head_dim).astype(f32)
    dmixing = jnp.einsum('qhd,khd->hqk', dattended, values)
    dvalues = jnp.einsum('hqk,qhd->khd', mixing_b.astype(f32), dattended)
    dscores = (mixing * (dmixing - lax.optimization_barrier(jnp.sum(mixing * dmixing, axis=2, keepdims=True))) * score_scale).astype(bf16)
    dqueries = jnp.einsum('hqk,khd->qhd', dscores.astype(f32), keys_all)
    dkeys = jnp.einsum('hqk,qhd->khd', dscores.astype(f32), queries)
    dprojected = jnp.stack([dqueries, dkeys, dvalues], axis=1).reshape(slot_count, 3 * D).astype(bf16)
    grad_project = jnp.dot(norm_in.T, dprojected, preferred_element_type=f32)
    dnorm = jnp.dot(dprojected, w_project.T, preferred_element_type=f32)
    grad_gain = lax.optimization_barrier(jnp.sum(dnorm * as_float * inverse, axis=0))
    scaled = dnorm * gain_f
    d_input = inverse * scaled - as_float * (inverse * inverse * inverse) * lax.optimization_barrier(jnp.mean(as_float * scaled, axis=1, keepdims=True)) + dhidden
    return (logits, d_input.astype(bf16), (grad_gain, grad_project, grad_out, grad_head))

def reference(packet_bytes, owner_index, session_id, class_label, byte_table, w_conv, norm_gain, w_project, w_out, w_head):
    f32 = jnp.float32
    bf16 = jnp.bfloat16
    devices = N_DP * N_REP
    capacity = 2 * PKT_DEV // N_DP
    slot_count = N_DP * capacity
    byte_codes = packet_bytes.reshape(devices, PKT_DEV, BYTES)
    owners = owner_index.reshape(devices, PKT_DEV)
    sessions = session_id.reshape(devices, PKT_DEV)
    chosen = (owners[:, :, None] == jnp.arange(N_DP, dtype=jnp.int32)[None, None, :]).astype(jnp.int32)
    send_rank = lax.optimization_barrier(jnp.sum((jnp.cumsum(chosen, axis=1) - 1) * chosen, axis=2)).astype(jnp.int32)
    device_ids = jnp.arange(devices, dtype=jnp.int32)
    dest_device = (owners * N_REP + (device_ids % N_REP)[:, None]).astype(jnp.int32)
    recv_slot = ((device_ids // N_REP)[:, None] * capacity + send_rank).astype(jnp.int32)

    def embed_device(codes_here):
        windows = windows_of(codes_here, byte_table)
        conv = jnp.dot(windows.reshape(-1, KERNEL * CHAN), w_conv, preferred_element_type=f32)
        conv = conv.reshape(PKT_DEV, POS, D)
        return lax.optimization_barrier(jnp.mean(jax.nn.silu(conv), axis=1)).astype(bf16)
    embedding = lax.map(embed_device, byte_codes)
    received = jnp.zeros((devices, slot_count, D), bf16).at[dest_device, recv_slot].set(embedding)
    recv_session = jnp.full((devices, slot_count), -1, jnp.int32).at[dest_device, recv_slot].set(sessions)
    labels_dev = class_label.reshape(devices, SESS)

    def owner_step(carry, item):
        received_here, session_here, labels_here = item
        logits_here, d_input, grads = session_layer(received_here, session_here, labels_here, norm_gain, w_project, w_out, w_head)
        return (tuple((total + part_grad for total, part_grad in zip(carry, grads))), (logits_here, d_input))
    start = (jnp.zeros((D,), f32), jnp.zeros((D, 3 * D), f32), jnp.zeros((D, D), f32), jnp.zeros((D, NCLS), f32))
    owner_totals, (logits, d_inputs) = lax.scan(owner_step, start, (received, recv_session, labels_dev))
    dembedding = d_inputs[dest_device, recv_slot]

    def source_step(carry, item):
        codes_here, demb_here = item
        windows = windows_of(codes_here, byte_table).reshape(-1, KERNEL * CHAN)
        conv = jnp.dot(windows, w_conv, preferred_element_type=f32).reshape(PKT_DEV, POS, D)
        dconv = (demb_here.astype(f32)[:, None, :] / POS * silu_slope(conv)).astype(bf16).reshape(-1, D)
        grad_conv = jnp.dot(windows.T, dconv, preferred_element_type=f32)
        dwindows = jnp.dot(dconv, w_conv.T, preferred_element_type=f32).astype(bf16).reshape(PKT_DEV * BYTES, CHAN)
        grad_table = jax.ops.segment_sum(dwindows.astype(f32), codes_here.reshape(-1), num_segments=256)
        return ((carry[0] + grad_table, carry[1] + grad_conv), None)
    cnn_start = (jnp.zeros((256, CHAN), f32), jnp.zeros((KERNEL * CHAN, D), f32))
    cnn_totals, unused = lax.scan(source_step, cnn_start, (byte_codes, dembedding))
    return (logits.reshape(devices * SESS, NCLS), cnn_totals[0], cnn_totals[1], owner_totals[0], owner_totals[1], owner_totals[2], owner_totals[3])
```

```python
import functools

import jax
import jax.numpy as jnp
from jax import lax
from jax.experimental import pallas as pl
from jax.experimental.pallas import tpu as pltpu
from jax.sharding import PartitionSpec as P

KERNEL = 8
HEADS = 8
NORM_EPS = 1e-06
WIN_STEP = 4
LANES = 128
VMEM_LIMIT = 56 * 2**20

f32 = jnp.float32
bf16 = jnp.bfloat16
AXES = ("dp", "rep")


def iota(shape, dim):
    return lax.broadcasted_iota(jnp.int32, shape, dim)


def dot_nn(a, b):
    return jnp.dot(a, b, preferred_element_type=f32)


def dot_nt(a, b):
    return lax.dot_general(a, b, (((1,), (1,)), ((), ())), preferred_element_type=f32)


def dot_tn(a, b):
    return lax.dot_general(a, b, (((0,), (0,)), ((), ())), preferred_element_type=f32)


def two_parts(value):
    high = value.astype(bf16)
    return high, (value - high.astype(f32)).astype(bf16)


def flag(mask):
    return jnp.where(mask, 1.0, 0.0).astype(bf16)


def embed_kernel(
    capacity, bytes_ref, own_row_ref, own_col_ref, sess_ref, table_ref, w_ref, out_ref, slope_ref, pair_ref, emb_ref
):
    step = pl.program_id(0)
    packets, length = bytes_ref.shape
    positions = length // KERNEL
    vocab, chan = table_ref.shape
    width = w_ref.shape[1]

    @pl.when(step == 0)
    def _():
        pair_ref[...] = jnp.zeros_like(pair_ref)
        pair_ref[0:vocab, 0:chan] = table_ref[...]
        pair_ref[vocab : 2 * vocab, chan : 2 * chan] = table_ref[...]
        emb_ref[...] = jnp.zeros_like(emb_ref)

    here = WIN_STEP * KERNEL
    codes = pltpu.roll(bytes_ref[...], lax.rem(length - here * step, length), 1)[:, :here]
    values = iota((packets, vocab), 1)
    pairs = []
    for k in range(KERNEL // 2):
        rows = []
        for w in range(WIN_STEP):
            j = w * KERNEL + 2 * k
            rows.append(
                jnp.concatenate([flag(codes[:, j : j + 1] == values), flag(codes[:, j + 1 : j + 2] == values)], axis=1)
            )
        pairs.append(dot_nn(jnp.concatenate(rows, axis=0), pair_ref[...]).astype(bf16))
    windows = jnp.concatenate(pairs, axis=1)
    conv = dot_nn(windows, w_ref[...])
    sigma = jax.nn.sigmoid(conv)
    act = conv * sigma
    slope_ref[...] = ((sigma + act * (1.0 - sigma)) * (1.0 / positions)).astype(bf16)
    total = emb_ref[...]
    for w in range(WIN_STEP):
        total += act[w * packets : (w + 1) * packets]
    emb_ref[...] = total

    @pl.when(step == pl.num_programs(0) - 1)
    def _():
        emb = (emb_ref[...] * (1.0 / positions)).astype(bf16)
        own_row = own_row_ref[...]
        same = (own_col_ref[...] == own_row) & (iota((packets, packets), 0) < iota((packets, packets), 1))
        rank = jnp.sum(jnp.where(same, 1.0, 0.0), axis=0, keepdims=True).astype(jnp.int32)
        place = flag(iota((out_ref.shape[0], packets), 0) == own_row * capacity + rank)
        out_ref[:, :width] = dot_nn(place, emb).astype(bf16)
        label = jnp.broadcast_to((sess_ref[...] + 1).astype(f32), (packets, LANES)).astype(bf16)
        out_ref[:, width:] = dot_nn(place, label).astype(bf16)


def embed(packet_bytes, own_row, own_col, sess_col, byte_table, w_conv, capacity, slots):
    packets, length = packet_bytes.shape
    rows = WIN_STEP * packets
    steps = length // (KERNEL * WIN_STEP)
    width = w_conv.shape[1]
    vocab, chan = byte_table.shape
    whole = lambda a: pl.BlockSpec(a.shape, lambda i: (0, 0))
    args = (packet_bytes, own_row, own_col, sess_col, byte_table, w_conv)
    return pl.pallas_call(
        functools.partial(embed_kernel, capacity),
        grid=(steps,),
        in_specs=[whole(a) for a in args],
        out_specs=[
            pl.BlockSpec((slots, width + LANES), lambda i: (0, 0)),
            pl.BlockSpec((rows, width), lambda i: (i, 0)),
        ],
        out_shape=[
            jax.ShapeDtypeStruct((slots, width + LANES), bf16),
            jax.ShapeDtypeStruct((steps * rows, width), bf16),
        ],
        scratch_shapes=[pltpu.VMEM((2 * vocab, 2 * chan), bf16), pltpu.VMEM((packets, width), f32)],
        compiler_params=pltpu.CompilerParams(vmem_limit_bytes=VMEM_LIMIT),
        name="embed",
    )(*args)


def session_kernel(
    inc_ref,
    label_ref,
    gain_ref,
    wp_ref,
    wo_ref,
    wh_ref,
    logits_ref,
    back_ref,
    early_ref,
    gain_grad_ref,
    proj_ref,
    att_ref,
    mix_ref,
    dproj_ref,
):
    slots = inc_ref.shape[0]
    width = wo_ref.shape[0]
    classes = wh_ref.shape[1]
    sessions = label_ref.shape[0]
    head = width // HEADS
    scale = head**-0.5

    embedding = inc_ref[:, :width]
    x = embedding.astype(f32)
    tags = inc_ref[:, width:].astype(f32)
    tag_col = tags[:, 0:1]
    tag_row = tags.T[0:1, :]
    gain = gain_ref[...].astype(f32)
    inverse = lax.rsqrt(jnp.mean(x * x, axis=1, keepdims=True) + NORM_EPS)
    norm_in = (x * inverse * gain).astype(bf16)
    proj_ref[...] = dot_nn(norm_in, wp_ref[...]).astype(bf16)

    def part(ref, which, h):
        at = which * width + h * head
        return ref[:, at : at + head]

    same = tag_col == tag_row
    for h in range(HEADS):
        scores = dot_nt(part(proj_ref, 0, h), part(proj_ref, 1, h)) * scale
        scores = jnp.where(same, scores, -1e30)
        shifted = jnp.exp(scores - jnp.max(scores, axis=1, keepdims=True))
        mixing = shifted / jnp.sum(shifted, axis=1, keepdims=True)
        mix_ref[h] = mixing
        att_ref[:, h * head : (h + 1) * head] = dot_nn(mixing.astype(bf16), part(proj_ref, 2, h)).astype(bf16)

    is_member = tag_row == (iota((sessions, slots), 0) + 1).astype(f32)
    member = flag(is_member)
    member_t = flag(tag_col == (iota((slots, sessions), 1) + 1).astype(f32))
    counts = jnp.maximum(jnp.sum(jnp.where(is_member, 1.0, 0.0), axis=1, keepdims=True), 1.0)
    att_high, att_low = two_parts(dot_nn(member, att_ref[...]))
    out_sum = dot_nn(att_high, wo_ref[...]) + dot_nn(att_low, wo_ref[...])
    pooled_b = ((dot_nn(member, embedding) + out_sum) / counts).astype(bf16)
    logits = dot_nn(pooled_b, wh_ref[...])
    logits_ref[...] = logits
    grown = jnp.exp(logits - jnp.max(logits, axis=1, keepdims=True))
    probs = grown / jnp.sum(grown, axis=1, keepdims=True)
    target = jnp.where(label_ref[...] == iota((sessions, classes), 1), 1.0, 0.0)
    dlogits = (probs - target) * (1.0 / sessions)
    dl_high, dl_low = two_parts(dlogits)
    grad_head = dot_tn(pooled_b, dl_high) + dot_tn(pooled_b, dl_low)
    dpooled = dot_nt(dl_high, wh_ref[...]) + dot_nt(dl_low, wh_ref[...])
    dsess = dpooled / counts
    dsess_b, dsess_low = two_parts(dsess)
    dhidden = dot_nn(member_t, dsess_b) + dot_nn(member_t, dsess_low)
    grad_out = dot_tn(att_high, dsess_b) + dot_tn(att_low, dsess_b)
    datt_s = dot_nt(dsess_b, wo_ref[...]).astype(bf16)
    datt = dot_nn(member_t, datt_s).astype(bf16)

    for h in range(HEADS):
        cols = slice(h * head, (h + 1) * head)
        mixing = mix_ref[h]
        dmix_s = dot_nt(datt_s[:, cols], part(proj_ref, 2, h))
        dmixing = jnp.sum(jnp.where(is_member, dmix_s, 0.0), axis=0, keepdims=True)
        weighted = mixing * dmixing
        dscores = ((weighted - mixing * jnp.sum(weighted, axis=1, keepdims=True)) * scale).astype(bf16)
        dq = dot_nn(dscores, part(proj_ref, 1, h))
        dk = dot_tn(dscores, part(proj_ref, 0, h))
        dv = dot_tn(mixing.astype(bf16), datt[:, cols])
        for which, d in ((0, dq), (1, dk), (2, dv)):
            at = which * width + h * head
            dproj_ref[:, at : at + head] = d.astype(bf16)

    def put(at, block):
        for s in range(block.shape[1] // LANES):
            early_ref[at + s * width : at + (s + 1) * width, :] = block[:, s * LANES : (s + 1) * LANES].astype(bf16)
        return at + block.shape[1] // LANES * width

    at = 0
    for which in range(3):
        at = put(at, dot_tn(norm_in, dproj_ref[:, which * width : (which + 1) * width]))
    at = put(at, grad_out)
    put(at, grad_head)
    dnorm = dot_nt(dproj_ref[...], wp_ref[...])
    grad_gain = jnp.sum(dnorm * x * inverse, axis=0, keepdims=True)
    gain_grad_ref[...] = jnp.zeros_like(gain_grad_ref)
    for s in range(width // LANES):
        gain_grad_ref[s : s + 1, :] = grad_gain[:, s * LANES : (s + 1) * LANES]
    scaled = dnorm * gain
    slant = jnp.mean(x * scaled, axis=1, keepdims=True) * (inverse * inverse * inverse)
    back_ref[...] = (inverse * scaled - x * slant + dhidden).astype(bf16)


def session_layer(incoming, labels, gain, w_project, w_out, w_head):
    slots = incoming.shape[0]
    width = w_out.shape[0]
    sessions, classes = labels.shape[0], w_head.shape[1]
    early_rows = width * (3 * width + width + classes) // LANES
    args = (incoming, labels, gain, w_project, w_out, w_head)
    vmem = pl.BlockSpec(memory_space=pltpu.VMEM)
    return pl.pallas_call(
        session_kernel,
        in_specs=[vmem] * len(args),
        out_specs=[vmem] * 4,
        out_shape=[
            jax.ShapeDtypeStruct((sessions, classes), f32),
            jax.ShapeDtypeStruct((slots, width), bf16),
            jax.ShapeDtypeStruct((early_rows, LANES), bf16),
            jax.ShapeDtypeStruct((16, LANES), f32),
        ],
        scratch_shapes=[
            pltpu.VMEM((slots, 3 * width), bf16),
            pltpu.VMEM((slots, width), bf16),
            pltpu.VMEM((HEADS, slots, slots), f32),
            pltpu.VMEM((slots, 3 * width), bf16),
        ],
        compiler_params=pltpu.CompilerParams(vmem_limit_bytes=VMEM_LIMIT),
        name="session_layer",
    )(*args)


def conv_back_kernel(
    capacity,
    ret_ref,
    own_row_ref,
    own_col_ref,
    codes_ref,
    slope_ref,
    table_ref,
    w_ref,
    gain_grad_ref,
    late_ref,
    dconv_ref,
    table_grad_ref,
):
    j = pl.program_id(0)
    slots, width = ret_ref.shape
    packets = own_col_ref.shape[0]
    vocab, chan = table_ref.shape
    positions = codes_ref.shape[1]

    @pl.when(j == 0)
    def _():
        same = (own_col_ref[...] == own_row_ref[...]) & (iota((packets, packets), 1) < iota((packets, packets), 0))
        rank = jnp.sum(jnp.where(same, 1.0, 0.0), axis=1, keepdims=True).astype(jnp.int32)
        place = flag(iota((packets, slots), 1) == own_col_ref[...] * capacity + rank)
        demb = dot_nn(place, ret_ref[...])
        for w in range(positions):
            at = slice(w * packets, (w + 1) * packets)
            dconv_ref[at, :] = (demb * slope_ref[at, :].astype(f32)).astype(bf16)
        table_grad_ref[...] = jnp.zeros_like(table_grad_ref)
        late_ref[...] = jnp.zeros_like(late_ref)

    values = iota((vocab, packets), 0)
    onehot = jnp.concatenate([flag(codes_ref[0, w : w + 1, :] == values) for w in range(positions)], axis=1)
    by_value = dot_nn(onehot, dconv_ref[...]).astype(bf16)
    w_rows = w_ref[pl.ds(pl.multiple_of(j * chan, chan), chan), :]
    table_grad_ref[...] += dot_nt(by_value, w_rows)
    grad_rows = dot_tn(table_ref[...], by_value).astype(bf16)
    window = KERNEL * chan
    for s in range(width // LANES):
        at = pl.multiple_of(s * window + j * chan, chan)
        late_ref[pl.ds(at, chan), :] = grad_rows[:, s * LANES : (s + 1) * LANES]

    @pl.when(j == pl.num_programs(0) - 1)
    def _():
        at = width // LANES * window
        half = vocab * chan // LANES
        late_ref[at : at + half, 0:chan] = table_grad_ref[0:half, :].astype(bf16)
        late_ref[at : at + half, chan : 2 * chan] = table_grad_ref[half : 2 * half, :].astype(bf16)
        late_ref[at + half : at + half + 16, :] = gain_grad_ref[...].astype(bf16)


def conv_back(returned, own_row, own_col, codes, slope, byte_table, w_conv, gain_grad, capacity, late_rows):
    width = w_conv.shape[1]
    whole = lambda a: pl.BlockSpec(a.shape, lambda j: (0, 0))
    args = (returned, own_row, own_col, codes, slope, byte_table, w_conv, gain_grad)
    specs = [whole(a) if a.ndim == 2 else pl.BlockSpec((1, *a.shape[1:]), lambda j: (j, 0, 0)) for a in args]
    return pl.pallas_call(
        functools.partial(conv_back_kernel, capacity),
        grid=(KERNEL,),
        in_specs=specs,
        out_specs=pl.BlockSpec((late_rows, LANES), lambda j: (0, 0)),
        out_shape=jax.ShapeDtypeStruct((late_rows, LANES), bf16),
        scratch_shapes=[pltpu.VMEM(slope.shape, bf16), pltpu.VMEM(byte_table.shape, f32)],
        compiler_params=pltpu.CompilerParams(vmem_limit_bytes=VMEM_LIMIT),
        name="conv_back",
    )(*args)


class Levels:
    def __init__(self, n_dp, n_rep):
        self.count = n_dp * n_rep
        self.index = lax.axis_index("dp") * n_rep + lax.axis_index("rep")
        self.levels = []
        stride, left = 1, self.count
        for size in (2, *[4] * 8):
            while size > 1 and left % size:
                size //= 2
            if size > 1:
                self.levels.append((stride, size))
                stride, left = stride * size, left // size
        assert left == 1

    def place(self, level):
        stride, size = level
        return lax.rem(lax.div(self.index, stride), size)

    def swap(self, value, level, d):
        stride, size = level
        return lax.ppermute(value, AXES, [(i, i + ((i // stride % size ^ d) - i // stride % size) * stride) for i in range(self.count)])

    def scatter_sum(self, value, level):
        size = level[1]
        value = value.reshape(size, value.shape[0] // size, value.shape[1])
        mine = self.place(level)
        got = [self.swap(lax.dynamic_index_in_dim(value, mine ^ d, 0, keepdims=False), level, d) for d in range(1, size)]
        total = lax.dynamic_index_in_dim(value, mine, 0, keepdims=False).astype(f32)
        for g in got:
            total = total + g.astype(f32)
        return total.astype(bf16)

    def gather(self, value, level):
        size = level[1]
        mine = self.place(level)
        got = [self.swap(value, level, d) for d in range(1, size)]
        out = jnp.zeros((size, *value.shape), value.dtype)
        for d, g in enumerate([value, *got]):
            out = lax.dynamic_update_index_in_dim(out, g, mine ^ d, 0)
        return out.reshape(size * value.shape[0], value.shape[1])

    def all_sum(self, value):
        for level in self.levels:
            value = self.scatter_sum(value, level)
        for level in self.levels[::-1]:
            value = self.gather(value, level)
        return value


def body(packet_bytes, owner_index, session_id, class_label, byte_table, w_conv, norm_gain, w_project, w_out, w_head):
    groups = lax.axis_size("dp")
    devices = Levels(groups, lax.axis_size("rep"))
    packets, length = packet_bytes.shape
    slots = 2 * packets
    capacity = slots // groups
    positions = length // KERNEL
    width = w_conv.shape[1]
    window = w_conv.shape[0]
    vocab, chan = byte_table.shape
    classes = w_head.shape[1]

    own_row = owner_index.reshape(1, packets)
    own_col = owner_index.reshape(packets, 1)
    outgoing, slope = embed(
        packet_bytes, own_row, own_col, session_id.reshape(packets, 1), byte_table, w_conv, capacity, slots
    )

    def exchange(rows):
        return lax.all_to_all(
            rows.reshape(groups, capacity, rows.shape[1]), "dp", split_axis=0, concat_axis=0, tiled=True
        ).reshape(rows.shape)

    logits, back, early, gain_grad = session_layer(
        exchange(outgoing), class_label.reshape(-1, 1), norm_gain.reshape(1, width), w_project, w_out, w_head
    )
    codes = packet_bytes.reshape(packets, positions, KERNEL).transpose(2, 1, 0)
    used = width // LANES * window + vocab * chan // LANES + 16
    unit = 8 * devices.count
    late_rows = -(-used // unit) * unit
    late = conv_back(
        exchange(back), own_row, own_col, codes, slope, byte_table, w_conv, gain_grad, capacity, late_rows
    )
    early = devices.all_sum(early).astype(f32)
    late = devices.all_sum(late).astype(f32)

    def take(rows, at, height, blocks):
        return rows[at : at + height * blocks].reshape(blocks, height, LANES).transpose(1, 0, 2).reshape(height, -1)

    wide = width // LANES
    grad_project = take(early, 0, width, 3 * wide)
    grad_out = take(early, 3 * wide * width, width, wide)
    grad_head = take(early, 4 * wide * width, width, classes // LANES)
    grad_conv = take(late, 0, window, wide)
    at = wide * window
    half = vocab * chan // LANES
    grad_table = jnp.concatenate([late[at : at + half, :chan], late[at : at + half, chan : 2 * chan]], axis=0)
    grad_gain = late[at + half : at + half + wide].reshape(width)
    return (logits, grad_table, grad_conv, grad_gain, grad_project, grad_out, grad_head)


def solution(mesh):
    split = P(AXES)
    rows = P(AXES, None)
    in_specs = (rows, split, split, split, P(), P(), P(), P(), P(), P())
    out_specs = (rows, P(), P(), P(), P(), P(), P())
    return jax.shard_map(body, mesh=mesh, in_specs=in_specs, out_specs=out_specs, check_vma=False)
```

```python
import functools

import jax
import jax.numpy as jnp
from jax import lax
from jax.experimental import pallas as pl
from jax.experimental.pallas import tpu as pltpu
from jax.sharding import PartitionSpec as P

KERNEL = 8
HEADS = 8
NORM_EPS = 1e-06
WIN_STEP = 4
LANES = 128
VMEM_LIMIT = 56 * 2**20

f32 = jnp.float32
bf16 = jnp.bfloat16
AXES = ("dp", "rep")


def iota(shape, dim):
    return lax.broadcasted_iota(jnp.int32, shape, dim)


def dot_nn(a, b):
    return jnp.dot(a, b, preferred_element_type=f32)


def dot_nt(a, b):
    return lax.dot_general(a, b, (((1,), (1,)), ((), ())), preferred_element_type=f32)


def dot_tn(a, b):
    return lax.dot_general(a, b, (((0,), (0,)), ((), ())), preferred_element_type=f32)


def two_parts(value):
    high = value.astype(bf16)
    return high, (value - high.astype(f32)).astype(bf16)


def flag(mask):
    return jnp.where(mask, 1.0, 0.0).astype(bf16)


def spread(row, lanes):
    return jnp.broadcast_to(row.astype(f32), (lanes, row.shape[1])).T


def column(row):
    return spread(row, LANES)[:, 0:1].astype(jnp.int32)


def cost(flops, moved):
    return pl.CostEstimate(flops=int(flops), bytes_accessed=int(moved), transcendentals=0)


def embed_kernel(
    capacity, bytes_ref, owner_ref, sess_ref, table_ref, w_ref, out_ref, slope_ref, pair_ref, emb_ref
):
    step = pl.program_id(0)
    packets, length = bytes_ref.shape
    positions = length // KERNEL
    chan, vocab = table_ref.shape
    width = w_ref.shape[1]

    @pl.when(step == 0)
    def _():
        table = table_ref[...].astype(f32).T.astype(bf16)
        pair_ref[...] = jnp.zeros_like(pair_ref)
        pair_ref[0:vocab, 0:chan] = table
        pair_ref[vocab : 2 * vocab, chan : 2 * chan] = table
        emb_ref[...] = jnp.zeros_like(emb_ref)

    here = WIN_STEP * KERNEL
    codes = pltpu.roll(bytes_ref[...], lax.rem(length - here * step, length), 1)[:, :here]
    values = iota((packets, vocab), 1)
    pairs = []
    for k in range(KERNEL // 2):
        rows = []
        for w in range(WIN_STEP):
            j = w * KERNEL + 2 * k
            rows.append(
                jnp.concatenate([flag(codes[:, j : j + 1] == values), flag(codes[:, j + 1 : j + 2] == values)], axis=1)
            )
        pairs.append(dot_nn(jnp.concatenate(rows, axis=0), pair_ref[...]).astype(bf16))
    windows = jnp.concatenate(pairs, axis=1)
    conv = dot_nn(windows, w_ref[...])
    sigma = jax.nn.sigmoid(conv)
    act = conv * sigma
    slope_ref[...] = ((sigma + act * (1.0 - sigma)) * (1.0 / positions)).astype(bf16)
    total = emb_ref[...]
    for w in range(WIN_STEP):
        total += act[w * packets : (w + 1) * packets]
    emb_ref[...] = total

    @pl.when(step == pl.num_programs(0) - 1)
    def _():
        emb = (emb_ref[...] * (1.0 / positions)).astype(bf16)
        own_row = owner_ref[...]
        same = (column(own_row) == own_row) & (iota((packets, packets), 0) < iota((packets, packets), 1))
        rank = jnp.sum(jnp.where(same, 1.0, 0.0), axis=0, keepdims=True).astype(jnp.int32)
        place = flag(iota((out_ref.shape[0], packets), 0) == own_row * capacity + rank)
        out_ref[:, :width] = dot_nn(place, emb).astype(bf16)
        label = spread(sess_ref[...] + 1, LANES).astype(bf16)
        out_ref[:, width:] = dot_nn(place, label).astype(bf16)


def embed(packet_bytes, owner, session, table_t, w_conv, capacity, slots):
    packets, length = packet_bytes.shape
    rows = WIN_STEP * packets
    steps = length // (KERNEL * WIN_STEP)
    width = w_conv.shape[1]
    chan, vocab = table_t.shape
    whole = lambda a: pl.BlockSpec(a.shape, lambda i: (0, 0))
    args = (packet_bytes, owner, session, table_t, w_conv)
    return pl.pallas_call(
        functools.partial(embed_kernel, capacity),
        grid=(steps,),
        in_specs=[whole(a) for a in args],
        out_specs=[
            pl.BlockSpec((slots, width + LANES), lambda i: (0, 0)),
            pl.BlockSpec((rows, width), lambda i: (i, 0)),
        ],
        out_shape=[
            jax.ShapeDtypeStruct((slots, width + LANES), bf16),
            jax.ShapeDtypeStruct((steps * rows, width), bf16),
        ],
        scratch_shapes=[pltpu.VMEM((2 * vocab, 2 * chan), bf16), pltpu.VMEM((packets, width), f32)],
        compiler_params=pltpu.CompilerParams(vmem_limit_bytes=VMEM_LIMIT),
        cost_estimate=cost(1e10, 5e6),
        name="embed",
    )(*args)


def share_out(core_ref, halves_ref, keep_ref, send_ref):
    mine = core_ref[0]
    keep_ref[...] = halves_ref[mine]
    send_ref[...] = halves_ref[1 - mine]


def session_kernel(
    core_ref,
    inc_ref,
    label_ref,
    gain_ref,
    wp_ref,
    wo_ref,
    wh_ref,
    logits_ref,
    back_ref,
    keep_ref,
    send_ref,
    gain_grad_ref,
    proj_ref,
    att_ref,
    mix_ref,
    dproj_ref,
    halves_ref,
):
    slots = inc_ref.shape[0]
    width = wo_ref.shape[0]
    classes = wh_ref.shape[1]
    sessions = logits_ref.shape[0]
    head = width // HEADS
    scale = head**-0.5

    embedding = inc_ref[:, :width]
    x = embedding.astype(f32)
    tags = inc_ref[:, width:].astype(f32)
    tag_col = tags[:, 0:1]
    tag_row = tags.T[0:1, :]
    gain = gain_ref[...].astype(f32)
    inverse = lax.rsqrt(jnp.mean(x * x, axis=1, keepdims=True) + NORM_EPS)
    norm_in = (x * inverse * gain).astype(bf16)
    proj_ref[...] = dot_nn(norm_in, wp_ref[...]).astype(bf16)

    def part(ref, which, h):
        at = which * width + h * head
        return ref[:, at : at + head]

    same = tag_col == tag_row
    for h in range(HEADS):
        scores = dot_nt(part(proj_ref, 0, h), part(proj_ref, 1, h)) * scale
        scores = jnp.where(same, scores, -1e30)
        shifted = jnp.exp(scores - jnp.max(scores, axis=1, keepdims=True))
        mixing = shifted / jnp.sum(shifted, axis=1, keepdims=True)
        mix_ref[h] = mixing
        att_ref[:, h * head : (h + 1) * head] = dot_nn(mixing.astype(bf16), part(proj_ref, 2, h)).astype(bf16)

    is_member = tag_row == (iota((sessions, slots), 0) + 1).astype(f32)
    member = flag(is_member)
    member_t = flag(tag_col == (iota((slots, sessions), 1) + 1).astype(f32))
    counts = jnp.maximum(jnp.sum(jnp.where(is_member, 1.0, 0.0), axis=1, keepdims=True), 1.0)
    att_high, att_low = two_parts(dot_nn(member, att_ref[...]))
    out_sum = dot_nn(att_high, wo_ref[...]) + dot_nn(att_low, wo_ref[...])
    pooled_b = ((dot_nn(member, embedding) + out_sum) / counts).astype(bf16)
    logits = dot_nn(pooled_b, wh_ref[...])
    logits_ref[...] = logits
    grown = jnp.exp(logits - jnp.max(logits, axis=1, keepdims=True))
    probs = grown / jnp.sum(grown, axis=1, keepdims=True)
    target = jnp.where(column(label_ref[...])[:sessions] == iota((sessions, classes), 1), 1.0, 0.0)
    dlogits = (probs - target) * (1.0 / sessions)
    dl_high, dl_low = two_parts(dlogits)
    grad_head = dot_tn(pooled_b, dl_high) + dot_tn(pooled_b, dl_low)
    dpooled = dot_nt(dl_high, wh_ref[...]) + dot_nt(dl_low, wh_ref[...])
    dsess = dpooled / counts
    dsess_b, dsess_low = two_parts(dsess)
    dhidden = dot_nn(member_t, dsess_b) + dot_nn(member_t, dsess_low)
    grad_out = dot_tn(att_high, dsess_b) + dot_tn(att_low, dsess_b)
    datt_s = dot_nt(dsess_b, wo_ref[...]).astype(bf16)
    datt = dot_nn(member_t, datt_s).astype(bf16)

    for h in range(HEADS):
        cols = slice(h * head, (h + 1) * head)
        mixing = mix_ref[h]
        dmix_s = dot_nt(datt_s[:, cols], part(proj_ref, 2, h))
        dmixing = jnp.sum(jnp.where(is_member, dmix_s, 0.0), axis=0, keepdims=True)
        weighted = mixing * dmixing
        dscores = ((weighted - mixing * jnp.sum(weighted, axis=1, keepdims=True)) * scale).astype(bf16)
        dq = dot_nn(dscores, part(proj_ref, 1, h))
        dk = dot_tn(dscores, part(proj_ref, 0, h))
        dv = dot_tn(mixing.astype(bf16), datt[:, cols])
        for which, d in ((0, dq), (1, dk), (2, dv)):
            at = which * width + h * head
            dproj_ref[:, at : at + head] = d.astype(bf16)

    at = [0, 0]

    def put(half, block):
        for s in range(block.shape[1] // LANES):
            rows = block.shape[0]
            halves_ref[half, at[half] : at[half] + rows, :] = block[:, s * LANES : (s + 1) * LANES].astype(bf16)
            at[half] += rows

    side = 3 * width // 2
    for half in range(2):
        put(half, dot_tn(norm_in, dproj_ref[:, half * side : (half + 1) * side]))
        put(half, grad_out[:, half * width // 2 : (half + 1) * width // 2])
        put(half, grad_head[half * width // 2 : (half + 1) * width // 2, :])
    share_out(core_ref, halves_ref, keep_ref, send_ref)
    dnorm = dot_nt(dproj_ref[...], wp_ref[...])
    grad_gain = jnp.sum(dnorm * x * inverse, axis=0, keepdims=True)
    gain_grad_ref[...] = jnp.zeros_like(gain_grad_ref)
    for s in range(width // LANES):
        gain_grad_ref[s : s + 1, :] = grad_gain[:, s * LANES : (s + 1) * LANES]
    scaled = dnorm * gain
    slant = jnp.mean(x * scaled, axis=1, keepdims=True) * (inverse * inverse * inverse)
    back_ref[...] = (inverse * scaled - x * slant + dhidden).astype(bf16)


def session_layer(core, incoming, labels, gain, w_project, w_out, w_head, sessions):
    slots = incoming.shape[0]
    width = w_out.shape[0]
    classes = w_head.shape[1]
    half_rows = width * (3 * width + width + classes) // (2 * LANES)
    args = (core, incoming, labels, gain, w_project, w_out, w_head)
    vmem = pl.BlockSpec(memory_space=pltpu.VMEM)
    half = jax.ShapeDtypeStruct((half_rows, LANES), bf16)
    return pl.pallas_call(
        session_kernel,
        in_specs=[pl.BlockSpec(memory_space=pltpu.SMEM)] + [vmem] * (len(args) - 1),
        out_specs=[vmem] * 5,
        out_shape=[
            jax.ShapeDtypeStruct((sessions, classes), f32),
            jax.ShapeDtypeStruct((slots, width), bf16),
            half,
            half,
            jax.ShapeDtypeStruct((16, LANES), f32),
        ],
        scratch_shapes=[
            pltpu.VMEM((slots, 3 * width), bf16),
            pltpu.VMEM((slots, width), bf16),
            pltpu.VMEM((HEADS, slots, slots), f32),
            pltpu.VMEM((slots, 3 * width), bf16),
            pltpu.VMEM((2, half_rows, LANES), bf16),
        ],
        compiler_params=pltpu.CompilerParams(vmem_limit_bytes=VMEM_LIMIT),
        cost_estimate=cost(1e10, 5e6),
        name="session_layer",
    )(*args)


def conv_back_kernel(
    capacity,
    core_ref,
    ret_ref,
    owner_ref,
    codes_ref,
    slope_ref,
    table_ref,
    w_ref,
    gain_grad_ref,
    keep_ref,
    send_ref,
    dconv_ref,
    table_grad_ref,
    halves_ref,
):
    j = pl.program_id(0)
    slots, width = ret_ref.shape
    packets = owner_ref.shape[1]
    chan, vocab = table_ref.shape
    positions = codes_ref.shape[1]

    @pl.when(j == 0)
    def _():
        own_row = owner_ref[...]
        own_col = column(own_row)
        same = (own_col == own_row) & (iota((packets, packets), 1) < iota((packets, packets), 0))
        rank = jnp.sum(jnp.where(same, 1.0, 0.0), axis=1, keepdims=True).astype(jnp.int32)
        place = flag(iota((packets, slots), 1) == own_col * capacity + rank)
        demb = dot_nn(place, ret_ref[...])
        for w in range(positions):
            at = slice(w * packets, (w + 1) * packets)
            dconv_ref[at, :] = (demb * slope_ref[at, :].astype(f32)).astype(bf16)
        table_grad_ref[...] = jnp.zeros_like(table_grad_ref)
        halves_ref[...] = jnp.zeros_like(halves_ref)

    values = iota((vocab, packets), 0)
    onehot = jnp.concatenate([flag(codes_ref[0, w : w + 1, :] == values) for w in range(positions)], axis=1)
    by_value = dot_nn(onehot, dconv_ref[...]).astype(bf16)
    w_rows = w_ref[pl.ds(pl.multiple_of(j * chan, chan), chan), :]
    table_grad_ref[...] += dot_nt(w_rows, by_value)
    grad_rows = dot_nn(table_ref[...], by_value).astype(bf16)
    window = KERNEL * chan
    wide = width // (2 * LANES)
    for half in range(2):
        for s in range(wide):
            at = pl.multiple_of(s * window + j * chan, chan)
            slab = half * wide + s
            halves_ref[half, pl.ds(at, chan), :] = grad_rows[:, slab * LANES : (slab + 1) * LANES]

    @pl.when(j == pl.num_programs(0) - 1)
    def _():
        at = wide * window
        for half in range(2):
            table_part = table_grad_ref[:, half * vocab // 2 : (half + 1) * vocab // 2]
            halves_ref[half, at : at + chan, :] = table_part.astype(bf16)
        halves_ref[0, at + chan : at + chan + 16, :] = gain_grad_ref[...].astype(bf16)
        share_out(core_ref, halves_ref, keep_ref, send_ref)


def conv_back(core, returned, owner, codes, slope, table_t, w_conv, gain_grad, capacity, half_rows):
    whole = lambda a: pl.BlockSpec(a.shape, lambda j: (0, 0))
    args = (returned, owner, codes, slope, table_t, w_conv, gain_grad)
    specs = [whole(a) if a.ndim == 2 else pl.BlockSpec((1, *a.shape[1:]), lambda j: (j, 0, 0)) for a in args]
    half = jax.ShapeDtypeStruct((half_rows, LANES), bf16)
    return pl.pallas_call(
        functools.partial(conv_back_kernel, capacity),
        grid=(KERNEL,),
        in_specs=[pl.BlockSpec(memory_space=pltpu.SMEM), *specs],
        out_specs=[whole(half), whole(half)],
        out_shape=[half, half],
        scratch_shapes=[
            pltpu.VMEM(slope.shape, bf16),
            pltpu.VMEM(table_t.shape, f32),
            pltpu.VMEM((2, half_rows, LANES), bf16),
        ],
        compiler_params=pltpu.CompilerParams(vmem_limit_bytes=VMEM_LIMIT),
        cost_estimate=cost(1e10, 5e6),
        name="conv_back",
    )(core, *args)


def put_together(place_ref, piece_refs, halves_ref):
    mine, k = place_ref[0], place_ref[1]
    rows = piece_refs[0].shape[0]
    count = len(piece_refs) // 2
    for i, ref in enumerate(piece_refs):
        half = mine if i < count else 1 - mine
        at = pl.multiple_of((k ^ (i % count)) * rows, 16)
        halves_ref[half, pl.ds(at, rows), :] = ref[...]


def early_out_kernel(place_ref, *refs):
    *pieces, project_ref, out_ref, head_ref, halves_ref = refs
    put_together(place_ref, pieces, halves_ref)
    for half in range(2):
        at = 0
        for ref in (project_ref, out_ref):
            rows, side = ref.shape[0], ref.shape[1] // 2
            for s in range(side // LANES):
                lanes = half * side + s * LANES
                ref[:, lanes : lanes + LANES] = halves_ref[half, at : at + rows, :].astype(f32)
                at += rows
        rows = head_ref.shape[0] // 2
        head_ref[half * rows : (half + 1) * rows, :] = halves_ref[half, at : at + rows, :].astype(f32)


def late_out_kernel(place_ref, *refs):
    *pieces, conv_ref, table_ref, gain_ref, halves_ref = refs
    put_together(place_ref, pieces, halves_ref)
    for half in range(2):
        at = 0
        rows, side = conv_ref.shape[0], conv_ref.shape[1] // 2
        for s in range(side // LANES):
            lanes = half * side + s * LANES
            conv_ref[:, lanes : lanes + LANES] = halves_ref[half, at : at + rows, :].astype(f32)
            at += rows
        chan, vocab = table_ref.shape
        table_ref[:, half * vocab // 2 : (half + 1) * vocab // 2] = halves_ref[half, at : at + chan, :].astype(f32)
        at += chan
        if half == 0:
            gain = halves_ref[0, at : at + 16, :].astype(f32)
            for s in range(gain_ref.shape[1] // LANES):
                gain_ref[:, s * LANES : (s + 1) * LANES] = gain[s : s + 1, :]


def assemble(kernel, place, pieces, shapes, name):
    vmem = pl.BlockSpec(memory_space=pltpu.VMEM)
    rows = len(pieces) // 2 * pieces[0].shape[0]
    return pl.pallas_call(
        kernel,
        in_specs=[pl.BlockSpec(memory_space=pltpu.SMEM)] + [vmem] * len(pieces),
        out_specs=[vmem] * len(shapes),
        out_shape=[jax.ShapeDtypeStruct(s, f32) for s in shapes],
        scratch_shapes=[pltpu.VMEM((2, rows, LANES), bf16)],
        compiler_params=pltpu.CompilerParams(vmem_limit_bytes=VMEM_LIMIT),
        cost_estimate=cost(1e9, 5e6),
        name=name,
    )(place, *pieces)


class Levels:
    def __init__(self, n_dp, n_rep):
        self.count = n_dp * n_rep
        self.index = lax.axis_index("dp") * n_rep + lax.axis_index("rep")
        self.levels = []
        stride, left = 1, self.count
        for size in (2, *[4] * 8):
            while size > 1 and left % size:
                size //= 2
            if size > 1:
                self.levels.append((stride, size))
                stride, left = stride * size, left // size
        assert left == 1

    def place(self, level):
        stride, size = level
        return lax.rem(lax.div(self.index, stride), size)

    def swap(self, value, level, d):
        stride, size = level
        return lax.ppermute(value, AXES, [(i, i + ((i // stride % size ^ d) - i // stride % size) * stride) for i in range(self.count)])

    def scatter_sum(self, value, level):
        size = level[1]
        value = value.reshape(size, value.shape[0] // size, value.shape[1])
        mine = self.place(level)
        got = [self.swap(lax.dynamic_index_in_dim(value, mine ^ d, 0, keepdims=False), level, d) for d in range(1, size)]
        total = lax.dynamic_index_in_dim(value, mine, 0, keepdims=False).astype(f32)
        for g in got:
            total = total + g.astype(f32)
        return total.astype(bf16)

    def gather(self, value, level):
        size = level[1]
        mine = self.place(level)
        got = [self.swap(value, level, d) for d in range(1, size)]
        out = jnp.zeros((size, *value.shape), value.dtype)
        for d, g in enumerate([value, *got]):
            out = lax.dynamic_update_index_in_dim(out, g, mine ^ d, 0)
        return out.reshape(size * value.shape[0], value.shape[1])

    def exchange_sum(self, value, level):
        terms = [value] + [self.swap(value, level, d) for d in range(1, level[1])]
        terms = [t.astype(f32) for t in terms]
        while len(terms) > 1:
            terms = [a + b for a, b in zip(terms[::2], terms[1::2], strict=True)]
        return terms[0].astype(bf16)

    def pair_sum(self, keep, send):
        return (keep.astype(f32) + self.swap(send, self.levels[0], 1).astype(f32)).astype(bf16)

    def pieces(self, value):
        quad = self.levels[1]
        own = [value] + [self.swap(value, quad, d) for d in range(1, quad[1])]
        return own + [self.swap(p, self.levels[0], 1) for p in own]


def body(packet_bytes, owner_index, session_id, class_label, byte_table, w_conv, norm_gain, w_project, w_out, w_head):
    groups = lax.axis_size("dp")
    devices = Levels(groups, lax.axis_size("rep"))
    packets, length = packet_bytes.shape
    slots = 2 * packets
    capacity = slots // groups
    positions = length // KERNEL
    width = w_conv.shape[1]
    window = w_conv.shape[0]
    vocab, chan = byte_table.shape
    classes = w_head.shape[1]
    sessions = class_label.shape[0]
    core = devices.place(devices.levels[0]).reshape(1)
    place = jnp.stack([devices.place(level) for level in devices.levels[:2]])

    owner = owner_index.reshape(1, packets)
    table_t = byte_table.T
    outgoing, slope = embed(packet_bytes, owner, session_id.reshape(1, packets), table_t, w_conv, capacity, slots)

    def exchange(rows):
        return lax.all_to_all(
            rows.reshape(groups, capacity, rows.shape[1]), "dp", split_axis=0, concat_axis=0, tiled=True
        ).reshape(rows.shape)

    logits, back, keep, send, gain_grad = session_layer(
        core,
        exchange(outgoing),
        class_label.reshape(1, sessions),
        norm_gain.reshape(1, width),
        w_project,
        w_out,
        w_head,
        sessions,
    )
    early = devices.pair_sum(keep, send)
    codes = packet_bytes.reshape(packets, positions, KERNEL).transpose(2, 1, 0)
    used = window * width // (2 * LANES) + chan * vocab // (2 * LANES) + 16
    unit = 64
    half_rows = -(-used // unit) * unit
    returned, early = lax.optimization_barrier((exchange(back), early))
    keep, send = conv_back(
        core, returned, owner, codes, slope, table_t, w_conv, gain_grad, capacity, half_rows
    )
    _, quad, *upper = devices.levels
    early = devices.scatter_sum(early, quad)
    for level in upper:
        early = devices.scatter_sum(early, level)
    for level in upper[::-1]:
        early = devices.gather(early, level)
    late = devices.scatter_sum(devices.pair_sum(keep, send), quad)
    for level in upper:
        late = devices.exchange_sum(late, level)
    grad_project, grad_out, grad_head = assemble(
        early_out_kernel, place, devices.pieces(early), [w_project.shape, w_out.shape, w_head.shape], "early_out"
    )
    grad_conv, table_grad, gain_grad = assemble(
        late_out_kernel, place, devices.pieces(late), [w_conv.shape, table_t.shape, (1, width)], "late_out"
    )
    return (logits, table_grad.T, grad_conv, gain_grad.reshape(width), grad_project, grad_out, grad_head)


def solution(mesh):
    split = P(AXES)
    rows = P(AXES, None)
    in_specs = (rows, split, split, split, P(), P(), P(), P(), P(), P())
    out_specs = (rows, P(), P(), P(), P(), P(), P())
    return jax.shard_map(body, mesh=mesh, in_specs=in_specs, out_specs=out_specs, check_vma=False)
```

```python
import functools

import jax
import jax.numpy as jnp
from jax import lax
from jax.experimental import pallas as pl
from jax.experimental.pallas import tpu as pltpu
from jax.sharding import PartitionSpec as P

KERNEL = 8
HEADS = 8
NORM_EPS = 1e-06
WIN_STEP = 8
LANES = 128
VMEM_LIMIT = 28 * 2**20

f32 = jnp.float32
bf16 = jnp.bfloat16
AXES = ("dp", "rep")


def iota(shape, dim):
    return lax.broadcasted_iota(jnp.int32, shape, dim)


def dot_nn(a, b):
    return jnp.dot(a, b, preferred_element_type=f32)


def dot_nt(a, b):
    return lax.dot_general(a, b, (((1,), (1,)), ((), ())), preferred_element_type=f32)


def dot_tn(a, b):
    return lax.dot_general(a, b, (((0,), (0,)), ((), ())), preferred_element_type=f32)


def two_parts(value):
    high = value.astype(bf16)
    return high, (value - high.astype(f32)).astype(bf16)


def flag(mask):
    return jnp.where(mask, 1.0, 0.0).astype(bf16)


def onehot(codes, values):
    return jnp.where(codes == values, jnp.ones((), bf16), jnp.zeros((), bf16))


def small_iota(shape, dim):
    return iota(shape, dim).astype(f32).astype(bf16)


def spread(row, lanes):
    return jnp.broadcast_to(row.astype(f32), (lanes, row.shape[1])).T


def column(row):
    return spread(row, LANES)[:, 0:1].astype(jnp.int32)


def cost(flops, moved):
    return pl.CostEstimate(flops=int(flops), bytes_accessed=int(moved), transcendentals=0)


def embed_kernel(
    capacity, bytes_ref, owner_ref, sess_ref, table_ref, w_ref, out_ref, slope_ref, pair_ref, emb_ref
):
    step = pl.program_id(0)
    packets, length = bytes_ref.shape
    positions = length // KERNEL
    chan, vocab = table_ref.shape
    width = w_ref.shape[1]

    @pl.when(step == 0)
    def _():
        table = table_ref[...].astype(f32).T.astype(bf16)
        pair_ref[...] = jnp.zeros_like(pair_ref)
        pair_ref[0:vocab, 0:chan] = table
        pair_ref[vocab : 2 * vocab, chan : 2 * chan] = table
        emb_ref[...] = jnp.zeros_like(emb_ref)

    here = WIN_STEP * KERNEL
    codes = pltpu.roll(bytes_ref[...], lax.rem(length - here * step, length), 1)[:, :here]
    codes = codes.astype(f32).astype(bf16)
    values = small_iota((packets, vocab), 1)
    pairs = []
    for k in range(KERNEL // 2):
        rows = []
        for w in range(WIN_STEP):
            j = w * KERNEL + 2 * k
            rows.append(
                jnp.concatenate([onehot(codes[:, j : j + 1], values), onehot(codes[:, j + 1 : j + 2], values)], axis=1)
            )
        pairs.append(dot_nn(jnp.concatenate(rows, axis=0), pair_ref[...]).astype(bf16))
    windows = jnp.concatenate(pairs, axis=1)
    conv = dot_nn(windows, w_ref[...])
    sigma = jax.nn.sigmoid(conv)
    act = conv * sigma
    slope_ref[...] = ((sigma + act * (1.0 - sigma)) * (1.0 / positions)).astype(bf16)
    total = emb_ref[...]
    for w in range(WIN_STEP):
        total += act[w * packets : (w + 1) * packets]
    emb_ref[...] = total

    @pl.when(step == pl.num_programs(0) - 1)
    def _():
        emb = (emb_ref[...] * (1.0 / positions)).astype(bf16)
        own_row = owner_ref[...]
        same = (column(own_row) == own_row) & (iota((packets, packets), 0) < iota((packets, packets), 1))
        rank = jnp.sum(jnp.where(same, 1.0, 0.0), axis=0, keepdims=True).astype(jnp.int32)
        place = flag(iota((out_ref.shape[0], packets), 0) == own_row * capacity + rank)
        out_ref[:, :width] = dot_nn(place, emb).astype(bf16)
        label = spread(sess_ref[...] + 1, LANES).astype(bf16)
        out_ref[:, width:] = dot_nn(place, label).astype(bf16)


def embed(packet_bytes, owner, session, table_t, w_conv, capacity, slots):
    packets, length = packet_bytes.shape
    rows = WIN_STEP * packets
    steps = length // (KERNEL * WIN_STEP)
    width = w_conv.shape[1]
    chan, vocab = table_t.shape
    whole = lambda a: pl.BlockSpec(a.shape, lambda i: (0, 0))
    args = (packet_bytes, owner, session, table_t, w_conv)
    return pl.pallas_call(
        functools.partial(embed_kernel, capacity),
        grid=(steps,),
        in_specs=[whole(a) for a in args],
        out_specs=[
            pl.BlockSpec((slots, width + LANES), lambda i: (0, 0)),
            pl.BlockSpec((rows, width), lambda i: (i, 0)),
        ],
        out_shape=[
            jax.ShapeDtypeStruct((slots, width + LANES), bf16),
            jax.ShapeDtypeStruct((steps * rows, width), bf16),
        ],
        scratch_shapes=[pltpu.VMEM((2 * vocab, 2 * chan), bf16), pltpu.VMEM((packets, width), f32)],
        compiler_params=pltpu.CompilerParams(vmem_limit_bytes=2 * VMEM_LIMIT),
        cost_estimate=cost(1e10, 5e6),
        name="embed",
    )(*args)


def share_out(core_ref, halves_ref, keep_ref, send_ref):
    mine = core_ref[0]
    keep_ref[...] = halves_ref[mine]
    send_ref[...] = halves_ref[1 - mine]


def session_kernel(
    core_ref,
    inc_ref,
    label_ref,
    gain_ref,
    wp_ref,
    wo_ref,
    wh_ref,
    logits_ref,
    back_ref,
    keep_ref,
    send_ref,
    gain_grad_ref,
    proj_ref,
    att_ref,
    mix_ref,
    dproj_ref,
    halves_ref,
):
    slots = inc_ref.shape[0]
    width = wo_ref.shape[0]
    classes = wh_ref.shape[1]
    sessions = logits_ref.shape[0]
    head = width // HEADS
    scale = head**-0.5

    embedding = inc_ref[:, :width]
    x = embedding.astype(f32)
    tags = inc_ref[:, width:].astype(f32)
    tag_col = tags[:, 0:1]
    tag_row = tags.T[0:1, :]
    gain = gain_ref[...].astype(f32)
    inverse = lax.rsqrt(jnp.mean(x * x, axis=1, keepdims=True) + NORM_EPS)
    norm_in = (x * inverse * gain).astype(bf16)
    proj_ref[...] = dot_nn(norm_in, wp_ref[...]).astype(bf16)

    def part(ref, which, h):
        at = which * width + h * head
        return ref[:, at : at + head]

    same = tag_col == tag_row
    for h in range(HEADS):
        scores = dot_nt(part(proj_ref, 0, h), part(proj_ref, 1, h)) * scale
        scores = jnp.where(same, scores, -1e30)
        shifted = jnp.exp(scores - jnp.max(scores, axis=1, keepdims=True))
        mixing = shifted / jnp.sum(shifted, axis=1, keepdims=True)
        mix_ref[h] = mixing
        att_ref[:, h * head : (h + 1) * head] = dot_nn(mixing.astype(bf16), part(proj_ref, 2, h)).astype(bf16)

    is_member = tag_row == (iota((sessions, slots), 0) + 1).astype(f32)
    member = flag(is_member)
    member_t = flag(tag_col == (iota((slots, sessions), 1) + 1).astype(f32))
    counts = jnp.maximum(jnp.sum(jnp.where(is_member, 1.0, 0.0), axis=1, keepdims=True), 1.0)
    att_high, att_low = two_parts(dot_nn(member, att_ref[...]))
    out_sum = dot_nn(att_high, wo_ref[...]) + dot_nn(att_low, wo_ref[...])
    pooled_b = ((dot_nn(member, embedding) + out_sum) / counts).astype(bf16)
    logits = dot_nn(pooled_b, wh_ref[...])
    logits_ref[...] = logits
    grown = jnp.exp(logits - jnp.max(logits, axis=1, keepdims=True))
    probs = grown / jnp.sum(grown, axis=1, keepdims=True)
    target = jnp.where(column(label_ref[...])[:sessions] == iota((sessions, classes), 1), 1.0, 0.0)
    dlogits = (probs - target) * (1.0 / sessions)
    dl_high, dl_low = two_parts(dlogits)
    grad_head = dot_tn(pooled_b, dl_high) + dot_tn(pooled_b, dl_low)
    dpooled = dot_nt(dl_high, wh_ref[...]) + dot_nt(dl_low, wh_ref[...])
    dsess = dpooled / counts
    dsess_b, dsess_low = two_parts(dsess)
    dhidden = dot_nn(member_t, dsess_b) + dot_nn(member_t, dsess_low)
    grad_out = dot_tn(att_high, dsess_b) + dot_tn(att_low, dsess_b)
    datt_s = dot_nt(dsess_b, wo_ref[...]).astype(bf16)
    datt = dot_nn(member_t, datt_s).astype(bf16)

    for h in range(HEADS):
        cols = slice(h * head, (h + 1) * head)
        mixing = mix_ref[h]
        dmix_s = dot_nt(datt_s[:, cols], part(proj_ref, 2, h))
        dmixing = jnp.sum(jnp.where(is_member, dmix_s, 0.0), axis=0, keepdims=True)
        weighted = mixing * dmixing
        dscores = ((weighted - mixing * jnp.sum(weighted, axis=1, keepdims=True)) * scale).astype(bf16)
        dq = dot_nn(dscores, part(proj_ref, 1, h))
        dk = dot_tn(dscores, part(proj_ref, 0, h))
        dv = dot_tn(mixing.astype(bf16), datt[:, cols])
        for which, d in ((0, dq), (1, dk), (2, dv)):
            at = which * width + h * head
            dproj_ref[:, at : at + head] = d.astype(bf16)

    at = [0, 0]

    def put(half, block):
        for s in range(block.shape[1] // LANES):
            rows = block.shape[0]
            halves_ref[half, at[half] : at[half] + rows, :] = block[:, s * LANES : (s + 1) * LANES].astype(bf16)
            at[half] += rows

    side = 3 * width // 2
    for half in range(2):
        put(half, dot_tn(norm_in, dproj_ref[:, half * side : (half + 1) * side]))
        put(half, grad_out[:, half * width // 2 : (half + 1) * width // 2])
        put(half, grad_head[half * width // 2 : (half + 1) * width // 2, :])
    share_out(core_ref, halves_ref, keep_ref, send_ref)
    dnorm = dot_nt(dproj_ref[...], wp_ref[...])
    grad_gain = jnp.sum(dnorm * x * inverse, axis=0, keepdims=True)
    gain_grad_ref[...] = jnp.zeros_like(gain_grad_ref)
    for s in range(width // LANES):
        gain_grad_ref[s : s + 1, :] = grad_gain[:, s * LANES : (s + 1) * LANES]
    scaled = dnorm * gain
    slant = jnp.mean(x * scaled, axis=1, keepdims=True) * (inverse * inverse * inverse)
    back_ref[...] = (inverse * scaled - x * slant + dhidden).astype(bf16)


def session_layer(core, incoming, labels, gain, w_project, w_out, w_head, sessions):
    slots = incoming.shape[0]
    width = w_out.shape[0]
    classes = w_head.shape[1]
    half_rows = width * (3 * width + width + classes) // (2 * LANES)
    args = (core, incoming, labels, gain, w_project, w_out, w_head)
    vmem = pl.BlockSpec(memory_space=pltpu.VMEM)
    half = jax.ShapeDtypeStruct((half_rows, LANES), bf16)
    return pl.pallas_call(
        session_kernel,
        in_specs=[pl.BlockSpec(memory_space=pltpu.SMEM)] + [vmem] * (len(args) - 1),
        out_specs=[vmem] * 5,
        out_shape=[
            jax.ShapeDtypeStruct((sessions, classes), f32),
            jax.ShapeDtypeStruct((slots, width), bf16),
            half,
            half,
            jax.ShapeDtypeStruct((16, LANES), f32),
        ],
        scratch_shapes=[
            pltpu.VMEM((slots, 3 * width), bf16),
            pltpu.VMEM((slots, width), bf16),
            pltpu.VMEM((HEADS, slots, slots), f32),
            pltpu.VMEM((slots, 3 * width), bf16),
            pltpu.VMEM((2, half_rows, LANES), bf16),
        ],
        compiler_params=pltpu.CompilerParams(vmem_limit_bytes=VMEM_LIMIT),
        cost_estimate=cost(1e10, 5e6),
        name="session_layer",
    )(*args)


def add_by_value(codes_ref, dconv_ref, table_ref, w_rows, table_grad_ref):
    packets = codes_ref.shape[2]
    vocab = table_ref.shape[1]
    values = small_iota((vocab, packets), 0)
    codes = codes_ref[0].astype(f32).astype(bf16)
    chosen = [onehot(codes[w : w + 1, :], values) for w in range(codes_ref.shape[1])]
    by_value = dot_nn(jnp.concatenate(chosen, axis=1), dconv_ref[...]).astype(bf16)
    table_grad_ref[...] += dot_nt(w_rows, by_value)
    return dot_nn(table_ref[...], by_value).astype(bf16)


def conv_back_kernel(
    capacity,
    ret_ref,
    owner_ref,
    codes_ref,
    slope_ref,
    table_ref,
    w_ref,
    dconv_ref,
    rows_ref,
    table_grad_ref,
):
    j = pl.program_id(0)
    slots, width = ret_ref.shape
    packets = owner_ref.shape[1]
    chan = table_ref.shape[0]

    @pl.when(j == 0)
    def _():
        own_row = owner_ref[...]
        own_col = column(own_row)
        same = (own_col == own_row) & (iota((packets, packets), 1) < iota((packets, packets), 0))
        rank = jnp.sum(jnp.where(same, 1.0, 0.0), axis=1, keepdims=True).astype(jnp.int32)
        place = flag(iota((packets, slots), 1) == own_col * capacity + rank)
        demb = dot_nn(place, ret_ref[...])
        for w in range(codes_ref.shape[1]):
            at = slice(w * packets, (w + 1) * packets)
            dconv_ref[at, :] = (demb * slope_ref[at, :].astype(f32)).astype(bf16)
        table_grad_ref[...] = jnp.zeros_like(table_grad_ref)

    at = pl.ds(pl.multiple_of(j * chan, chan), chan)
    rows_ref[at, :] = add_by_value(codes_ref, dconv_ref, table_ref, w_ref[at, :], table_grad_ref)


def conv_back_rest_kernel(
    core_ref,
    codes_ref,
    dconv_ref,
    table_ref,
    w_ref,
    first_rows_ref,
    first_table_ref,
    gain_grad_ref,
    keep_ref,
    send_ref,
    rows_ref,
    table_grad_ref,
    halves_ref,
):
    j = pl.program_id(0)
    width = dconv_ref.shape[1]
    chan, vocab = table_ref.shape
    window = w_ref.shape[0]
    done = first_rows_ref.shape[0]

    @pl.when(j == 0)
    def _():
        rows_ref[0:done, :] = first_rows_ref[...]
        table_grad_ref[...] = first_table_ref[...]
        halves_ref[...] = jnp.zeros_like(halves_ref)

    at = pl.ds(pl.multiple_of(done + j * chan, chan), chan)
    rows_ref[at, :] = add_by_value(codes_ref, dconv_ref, table_ref, w_ref[at, :], table_grad_ref)

    @pl.when(j == pl.num_programs(0) - 1)
    def _():
        wide = width // (2 * LANES)
        for half in range(2):
            for s in range(wide):
                slab = half * wide + s
                halves_ref[half, s * window : (s + 1) * window, :] = rows_ref[:, slab * LANES : (slab + 1) * LANES]
            end = wide * window
            table_part = table_grad_ref[:, half * vocab // 2 : (half + 1) * vocab // 2]
            halves_ref[half, end : end + chan, :] = table_part.astype(bf16)
        halves_ref[0, end + chan : end + chan + 16, :] = gain_grad_ref[...].astype(bf16)
        share_out(core_ref, halves_ref, keep_ref, send_ref)


def whole(a):
    return pl.BlockSpec(a.shape, lambda j: (0,) * len(a.shape))


def conv_back(returned, owner, codes, slope, table_t, w_conv, capacity, steps):
    args = (returned, owner, codes, slope, table_t, w_conv)
    chan = table_t.shape[0]
    specs = [whole(a) if a.ndim == 2 else pl.BlockSpec((1, *a.shape[1:]), lambda j: (j, 0, 0)) for a in args]
    outs = [
        jax.ShapeDtypeStruct(slope.shape, bf16),
        jax.ShapeDtypeStruct((steps * chan, w_conv.shape[1]), bf16),
        jax.ShapeDtypeStruct(table_t.shape, f32),
    ]
    return pl.pallas_call(
        functools.partial(conv_back_kernel, capacity),
        grid=(steps,),
        in_specs=specs,
        out_specs=[whole(o) for o in outs],
        out_shape=outs,
        compiler_params=pltpu.CompilerParams(vmem_limit_bytes=VMEM_LIMIT),
        cost_estimate=cost(8e9, 1e7),
        name="conv_back",
    )(*args)


def conv_back_rest(core, codes, dconv, table_t, w_conv, rows, table_grad, gain_grad, half_rows, first):
    args = (codes, dconv, table_t, w_conv, rows, table_grad, gain_grad)
    specs = [whole(a) if a.ndim == 2 else pl.BlockSpec((1, *a.shape[1:]), lambda j: (j + first, 0, 0)) for a in args]
    half = jax.ShapeDtypeStruct((half_rows, LANES), bf16)
    return pl.pallas_call(
        conv_back_rest_kernel,
        grid=(KERNEL - first,),
        in_specs=[pl.BlockSpec(memory_space=pltpu.SMEM), *specs],
        out_specs=[whole(half), whole(half)],
        out_shape=[half, half],
        scratch_shapes=[
            pltpu.VMEM(w_conv.shape, bf16),
            pltpu.VMEM(table_t.shape, f32),
            pltpu.VMEM((2, half_rows, LANES), bf16),
        ],
        compiler_params=pltpu.CompilerParams(vmem_limit_bytes=VMEM_LIMIT),
        cost_estimate=cost(6e9, 6e6),
        name="conv_back_rest",
    )(core, *args)


def put_together(place_ref, piece_refs, halves_ref):
    mine, k = place_ref[0], place_ref[1]
    rows = piece_refs[0].shape[0]
    count = len(piece_refs) // 2
    for i, ref in enumerate(piece_refs):
        half = mine if i < count else 1 - mine
        at = pl.multiple_of((k ^ (i % count)) * rows, 16)
        halves_ref[half, pl.ds(at, rows), :] = ref[...]


def early_out_kernel(place_ref, *refs):
    *pieces, project_ref, out_ref, head_ref, halves_ref = refs
    put_together(place_ref, pieces, halves_ref)
    for half in range(2):
        at = 0
        for ref in (project_ref, out_ref):
            rows, side = ref.shape[0], ref.shape[1] // 2
            for s in range(side // LANES):
                lanes = half * side + s * LANES
                ref[:, lanes : lanes + LANES] = halves_ref[half, at : at + rows, :].astype(f32)
                at += rows
        rows = head_ref.shape[0] // 2
        head_ref[half * rows : (half + 1) * rows, :] = halves_ref[half, at : at + rows, :].astype(f32)


def late_out_kernel(place_ref, *refs):
    *pieces, conv_ref, table_ref, gain_ref, halves_ref = refs
    put_together(place_ref, pieces, halves_ref)
    for half in range(2):
        at = 0
        rows, side = conv_ref.shape[0], conv_ref.shape[1] // 2
        for s in range(side // LANES):
            lanes = half * side + s * LANES
            conv_ref[:, lanes : lanes + LANES] = halves_ref[half, at : at + rows, :].astype(f32)
            at += rows
        chan, vocab = table_ref.shape
        table_ref[:, half * vocab // 2 : (half + 1) * vocab // 2] = halves_ref[half, at : at + chan, :].astype(f32)
        at += chan
        if half == 0:
            gain = halves_ref[0, at : at + 16, :].astype(f32)
            for s in range(gain_ref.shape[1] // LANES):
                gain_ref[:, s * LANES : (s + 1) * LANES] = gain[s : s + 1, :]


def assemble(kernel, place, pieces, shapes, name):
    vmem = pl.BlockSpec(memory_space=pltpu.VMEM)
    rows = len(pieces) // 2 * pieces[0].shape[0]
    return pl.pallas_call(
        kernel,
        in_specs=[pl.BlockSpec(memory_space=pltpu.SMEM)] + [vmem] * len(pieces),
        out_specs=[vmem] * len(shapes),
        out_shape=[jax.ShapeDtypeStruct(s, f32) for s in shapes],
        scratch_shapes=[pltpu.VMEM((2, rows, LANES), bf16)],
        compiler_params=pltpu.CompilerParams(vmem_limit_bytes=VMEM_LIMIT),
        cost_estimate=cost(1e9, 5e6),
        name=name,
    )(place, *pieces)


class Levels:
    def __init__(self, n_dp, n_rep):
        self.count = n_dp * n_rep
        self.index = lax.axis_index("dp") * n_rep + lax.axis_index("rep")
        self.levels = []
        stride, left = 1, self.count
        for size in (2, *[4] * 8):
            while size > 1 and left % size:
                size //= 2
            if size > 1:
                self.levels.append((stride, size))
                stride, left = stride * size, left // size
        assert left == 1

    def place(self, level):
        stride, size = level
        return lax.rem(lax.div(self.index, stride), size)

    def swap(self, value, level, d):
        stride, size = level
        return lax.ppermute(value, AXES, [(i, i + ((i // stride % size ^ d) - i // stride % size) * stride) for i in range(self.count)])

    def scatter_sum(self, value, level, other=None):
        size = level[1]
        value = value.reshape(size, value.shape[0] // size, value.shape[1])
        mine = self.place(level)
        got = [self.swap(lax.dynamic_index_in_dim(value, mine ^ d, 0, keepdims=False), level, d) for d in range(1, size)]
        if other is not None:
            got = after(got, other)
        total = lax.dynamic_index_in_dim(value, mine, 0, keepdims=False).astype(f32)
        for g in got:
            total = total + g.astype(f32)
        return total.astype(bf16)

    def gather(self, value, level):
        size = level[1]
        mine = self.place(level)
        got = [self.swap(value, level, d) for d in range(1, size)]
        out = jnp.zeros((size, *value.shape), value.dtype)
        for d, g in enumerate([value, *got]):
            out = lax.dynamic_update_index_in_dim(out, g, mine ^ d, 0)
        return out.reshape(size * value.shape[0], value.shape[1])

    def exchange_sum(self, value, level):
        terms = [value] + [self.swap(value, level, d) for d in range(1, level[1])]
        terms = [t.astype(f32) for t in terms]
        while len(terms) > 1:
            terms = [a + b for a, b in zip(terms[::2], terms[1::2], strict=True)]
        return terms[0].astype(bf16)

    def pair_sum(self, keep, send):
        return (keep.astype(f32) + self.swap(send, self.levels[0], 1).astype(f32)).astype(bf16)

    def pieces(self, value):
        quad = self.levels[1]
        own = [value] + [self.swap(value, quad, d) for d in range(1, quad[1])]
        return own + [self.swap(p, self.levels[0], 1) for p in own]


def after(value, other):
    return lax.optimization_barrier((value, other))[0]


def body(packet_bytes, owner_index, session_id, class_label, byte_table, w_conv, norm_gain, w_project, w_out, w_head):
    groups = lax.axis_size("dp")
    devices = Levels(groups, lax.axis_size("rep"))
    packets, length = packet_bytes.shape
    slots = 2 * packets
    capacity = slots // groups
    positions = length // KERNEL
    width = w_conv.shape[1]
    window = w_conv.shape[0]
    vocab, chan = byte_table.shape
    classes = w_head.shape[1]
    sessions = class_label.shape[0]
    core = devices.place(devices.levels[0]).reshape(1)
    place = jnp.stack([devices.place(level) for level in devices.levels[:2]])

    owner = owner_index.reshape(1, packets)
    table_t = byte_table.T
    outgoing, slope = embed(packet_bytes, owner, session_id.reshape(1, packets), table_t, w_conv, capacity, slots)

    def exchange(rows):
        return lax.all_to_all(
            rows.reshape(groups, capacity, rows.shape[1]), "dp", split_axis=0, concat_axis=0, tiled=True
        ).reshape(rows.shape)

    logits, back, keep, send, gain_grad = session_layer(
        core,
        exchange(outgoing),
        class_label.reshape(1, sessions),
        norm_gain.reshape(1, width),
        w_project,
        w_out,
        w_head,
        sessions,
    )
    early = devices.pair_sum(keep, send)
    codes = packet_bytes.reshape(packets, positions, KERNEL).transpose(2, 1, 0)
    used = window * width // (2 * LANES) + chan * vocab // (2 * LANES) + 16
    unit = 64
    half_rows = -(-used // unit) * unit
    first = KERNEL // 2
    _, quad, *upper = devices.levels
    dconv, rows, table_rows = conv_back(
        after(exchange(back), early), owner, codes, slope, table_t, w_conv, capacity, first
    )
    early = devices.scatter_sum(early, quad, rows)
    keep, send = conv_back_rest(
        core, codes, dconv, table_t, w_conv, rows, after(table_rows, early), gain_grad, half_rows, first
    )
    for level in upper:
        early = devices.scatter_sum(early, level, keep)
    for level in upper[::-1]:
        early = devices.gather(early, level)
    late = devices.scatter_sum(devices.pair_sum(keep, send), quad)
    for level in upper:
        late = devices.exchange_sum(late, level)
    grad_project, grad_out, grad_head = assemble(
        early_out_kernel, place, devices.pieces(early), [w_project.shape, w_out.shape, w_head.shape], "early_out"
    )
    grad_conv, table_grad, gain_grad = assemble(
        late_out_kernel, place, devices.pieces(late), [w_conv.shape, table_t.shape, (1, width)], "late_out"
    )
    return (logits, table_grad.T, grad_conv, gain_grad.reshape(width), grad_project, grad_out, grad_head)


def solution(mesh):
    split = P(AXES)
    rows = P(AXES, None)
    in_specs = (rows, split, split, split, P(), P(), P(), P(), P(), P())
    out_specs = (rows, P(), P(), P(), P(), P(), P())
    return jax.shard_map(body, mesh=mesh, in_specs=in_specs, out_specs=out_specs, check_vma=False)
```

```python
import functools

import jax
import jax.numpy as jnp
from jax import lax
from jax.experimental import pallas as pl
from jax.experimental.pallas import tpu as pltpu
from jax.sharding import PartitionSpec as P

KERNEL = 8
HEADS = 8
NORM_EPS = 1e-06
WIN_STEP = 8
SLOPE_PIECES = 4
LANES = 128
VMEM_LIMIT = 28 * 2**20

f32 = jnp.float32
bf16 = jnp.bfloat16
AXES = ("dp", "rep")


def iota(shape, dim):
    return lax.broadcasted_iota(jnp.int32, shape, dim)


def dot_nn(a, b):
    return jnp.dot(a, b, preferred_element_type=f32)


def dot_nt(a, b):
    return lax.dot_general(a, b, (((1,), (1,)), ((), ())), preferred_element_type=f32)


def dot_tn(a, b):
    return lax.dot_general(a, b, (((0,), (0,)), ((), ())), preferred_element_type=f32)


def two_parts(value):
    high = value.astype(bf16)
    return high, (value - high.astype(f32)).astype(bf16)


def flag(mask):
    return jnp.where(mask, 1.0, 0.0).astype(bf16)


def onehot(codes, values):
    return jnp.where(codes == values, jnp.ones((), bf16), jnp.zeros((), bf16))


def small_iota(shape, dim):
    return iota(shape, dim).astype(f32).astype(bf16)


def spread(row, lanes):
    return jnp.broadcast_to(row.astype(f32), (lanes, row.shape[1])).T


def column(row):
    return spread(row, LANES)[:, 0:1].astype(jnp.int32)


def cost(flops, moved):
    return pl.CostEstimate(flops=int(flops), bytes_accessed=int(moved), transcendentals=0)


def embed_kernel(
    capacity, bytes_ref, owner_ref, sess_ref, table_ref, w_ref, out_ref, slope_ref, codes_ref, pair_ref, emb_ref, turned_ref
):
    step = pl.program_id(0)
    packets, length = bytes_ref.shape
    positions = length // KERNEL
    chan, vocab = table_ref.shape
    width = w_ref.shape[1]

    @pl.when(step == 0)
    def _():
        table = table_ref[...].astype(f32).T.astype(bf16)
        pair_ref[...] = jnp.zeros_like(pair_ref)
        pair_ref[0:vocab, 0:chan] = table
        pair_ref[vocab : 2 * vocab, chan : 2 * chan] = table
        emb_ref[...] = jnp.zeros_like(emb_ref)
        turned_ref[...] = bytes_ref[...].astype(f32).T
        for j in range(KERNEL):
            codes_ref[j] = turned_ref[pl.ds(j, positions, stride=KERNEL), :].astype(bf16)

    here = WIN_STEP * KERNEL
    codes = pltpu.roll(bytes_ref[...], lax.rem(length - here * step, length), 1)[:, :here]
    codes = codes.astype(f32).astype(bf16)
    values = small_iota((packets, vocab), 1)
    pairs = []
    for k in range(KERNEL // 2):
        rows = []
        for w in range(WIN_STEP):
            j = w * KERNEL + 2 * k
            rows.append(
                jnp.concatenate([onehot(codes[:, j : j + 1], values), onehot(codes[:, j + 1 : j + 2], values)], axis=1)
            )
        pairs.append(dot_nn(jnp.concatenate(rows, axis=0), pair_ref[...]).astype(bf16))
    windows = jnp.concatenate(pairs, axis=1)
    conv = dot_nn(windows, w_ref[...])
    sigma = jax.nn.sigmoid(conv)
    act = conv * sigma
    slope_ref[...] = ((sigma + act * (1.0 - sigma)) * (1.0 / positions)).astype(bf16)
    total = emb_ref[...]
    for w in range(WIN_STEP):
        total += act[w * packets : (w + 1) * packets]
    emb_ref[...] = total

    @pl.when(step == pl.num_programs(0) - 1)
    def _():
        emb = (emb_ref[...] * (1.0 / positions)).astype(bf16)
        own_row = owner_ref[...]
        same = (column(own_row) == own_row) & (iota((packets, packets), 0) < iota((packets, packets), 1))
        rank = jnp.sum(jnp.where(same, 1.0, 0.0), axis=0, keepdims=True).astype(jnp.int32)
        place = flag(iota((out_ref.shape[0], packets), 0) == own_row * capacity + rank)
        out_ref[:, :width] = dot_nn(place, emb).astype(bf16)
        label = spread(sess_ref[...] + 1, LANES).astype(bf16)
        out_ref[:, width:] = dot_nn(place, label).astype(bf16)


def embed(packet_bytes, owner, session, table_t, w_conv, capacity, slots):
    packets, length = packet_bytes.shape
    rows = WIN_STEP * packets
    steps = length // (KERNEL * WIN_STEP)
    width = w_conv.shape[1]
    chan, vocab = table_t.shape
    whole = lambda a: pl.BlockSpec(a.shape, lambda i: (0, 0))
    args = (packet_bytes, owner, session, table_t, w_conv)
    return pl.pallas_call(
        functools.partial(embed_kernel, capacity),
        grid=(steps,),
        in_specs=[whole(a) for a in args],
        out_specs=[
            pl.BlockSpec((slots, width + LANES), lambda i: (0, 0)),
            pl.BlockSpec((rows, width), lambda i: (i, 0)),
            pl.BlockSpec((KERNEL, length // KERNEL, packets), lambda i: (0, 0, 0)),
        ],
        out_shape=[
            jax.ShapeDtypeStruct((slots, width + LANES), bf16),
            jax.ShapeDtypeStruct((steps * rows, width), bf16),
            jax.ShapeDtypeStruct((KERNEL, length // KERNEL, packets), bf16),
        ],
        scratch_shapes=[
            pltpu.VMEM((2 * vocab, 2 * chan), bf16),
            pltpu.VMEM((packets, width), f32),
            pltpu.VMEM((length, packets), f32),
        ],
        compiler_params=pltpu.CompilerParams(vmem_limit_bytes=2 * VMEM_LIMIT),
        cost_estimate=cost(1e10, 5e6),
        name="embed",
    )(*args)


def share_out(core_ref, halves_ref, keep_ref, send_ref):
    mine = core_ref[0]
    keep_ref[...] = halves_ref[mine]
    send_ref[...] = halves_ref[1 - mine]


def session_kernel(
    core_ref,
    inc_ref,
    label_ref,
    gain_ref,
    wp_ref,
    wo_ref,
    wh_ref,
    logits_ref,
    back_ref,
    keep_ref,
    send_ref,
    gain_grad_ref,
    proj_ref,
    att_ref,
    mix_ref,
    dproj_ref,
    halves_ref,
):
    slots = inc_ref.shape[0]
    width = wo_ref.shape[0]
    classes = wh_ref.shape[1]
    sessions = logits_ref.shape[0]
    head = width // HEADS
    scale = head**-0.5

    embedding = inc_ref[:, :width]
    x = embedding.astype(f32)
    tags = inc_ref[:, width:].astype(f32)
    tag_col = tags[:, 0:1]
    tag_row = tags.T[0:1, :]
    gain = gain_ref[...].astype(f32)
    inverse = lax.rsqrt(jnp.mean(x * x, axis=1, keepdims=True) + NORM_EPS)
    norm_in = (x * inverse * gain).astype(bf16)
    proj_ref[...] = dot_nn(norm_in, wp_ref[...]).astype(bf16)

    def part(ref, which, h):
        at = which * width + h * head
        return ref[:, at : at + head]

    same = tag_col == tag_row
    for h in range(HEADS):
        scores = dot_nt(part(proj_ref, 0, h), part(proj_ref, 1, h)) * scale
        scores = jnp.where(same, scores, -1e30)
        shifted = jnp.exp(scores - jnp.max(scores, axis=1, keepdims=True))
        mixing = shifted / jnp.sum(shifted, axis=1, keepdims=True)
        mix_ref[h] = mixing
        att_ref[:, h * head : (h + 1) * head] = dot_nn(mixing.astype(bf16), part(proj_ref, 2, h)).astype(bf16)

    is_member = tag_row == (iota((sessions, slots), 0) + 1).astype(f32)
    member = flag(is_member)
    member_t = flag(tag_col == (iota((slots, sessions), 1) + 1).astype(f32))
    counts = jnp.maximum(jnp.sum(jnp.where(is_member, 1.0, 0.0), axis=1, keepdims=True), 1.0)
    att_high, att_low = two_parts(dot_nn(member, att_ref[...]))
    out_sum = dot_nn(att_high, wo_ref[...]) + dot_nn(att_low, wo_ref[...])
    pooled_b = ((dot_nn(member, embedding) + out_sum) / counts).astype(bf16)
    logits = dot_nn(pooled_b, wh_ref[...])
    logits_ref[...] = logits
    grown = jnp.exp(logits - jnp.max(logits, axis=1, keepdims=True))
    probs = grown / jnp.sum(grown, axis=1, keepdims=True)
    target = jnp.where(column(label_ref[...])[:sessions] == iota((sessions, classes), 1), 1.0, 0.0)
    dlogits = (probs - target) * (1.0 / sessions)
    dl_high, dl_low = two_parts(dlogits)
    grad_head = dot_tn(pooled_b, dl_high) + dot_tn(pooled_b, dl_low)
    dpooled = dot_nt(dl_high, wh_ref[...]) + dot_nt(dl_low, wh_ref[...])
    dsess = dpooled / counts
    dsess_b, dsess_low = two_parts(dsess)
    dhidden = dot_nn(member_t, dsess_b) + dot_nn(member_t, dsess_low)
    grad_out = dot_tn(att_high, dsess_b) + dot_tn(att_low, dsess_b)
    datt_s = dot_nt(dsess_b, wo_ref[...]).astype(bf16)
    datt = dot_nn(member_t, datt_s).astype(bf16)

    for h in range(HEADS):
        cols = slice(h * head, (h + 1) * head)
        mixing = mix_ref[h]
        dmix_s = dot_nt(datt_s[:, cols], part(proj_ref, 2, h))
        dmixing = jnp.sum(jnp.where(is_member, dmix_s, 0.0), axis=0, keepdims=True)
        weighted = mixing * dmixing
        dscores = ((weighted - mixing * jnp.sum(weighted, axis=1, keepdims=True)) * scale).astype(bf16)
        dq = dot_nn(dscores, part(proj_ref, 1, h))
        dk = dot_tn(dscores, part(proj_ref, 0, h))
        dv = dot_tn(mixing.astype(bf16), datt[:, cols])
        for which, d in ((0, dq), (1, dk), (2, dv)):
            at = which * width + h * head
            dproj_ref[:, at : at + head] = d.astype(bf16)

    at = [0, 0]

    def put(half, block):
        for s in range(block.shape[1] // LANES):
            rows = block.shape[0]
            halves_ref[half, at[half] : at[half] + rows, :] = block[:, s * LANES : (s + 1) * LANES].astype(bf16)
            at[half] += rows

    side = 3 * width // 2
    for half in range(2):
        put(half, dot_tn(norm_in, dproj_ref[:, half * side : (half + 1) * side]))
        put(half, grad_out[:, half * width // 2 : (half + 1) * width // 2])
        put(half, grad_head[half * width // 2 : (half + 1) * width // 2, :])
    share_out(core_ref, halves_ref, keep_ref, send_ref)
    dnorm = dot_nt(dproj_ref[...], wp_ref[...])
    grad_gain = jnp.sum(dnorm * x * inverse, axis=0, keepdims=True)
    gain_grad_ref[...] = jnp.zeros_like(gain_grad_ref)
    for s in range(width // LANES):
        gain_grad_ref[s : s + 1, :] = grad_gain[:, s * LANES : (s + 1) * LANES]
    scaled = dnorm * gain
    slant = jnp.mean(x * scaled, axis=1, keepdims=True) * (inverse * inverse * inverse)
    back_ref[...] = (inverse * scaled - x * slant + dhidden).astype(bf16)


def session_layer(core, incoming, labels, gain, w_project, w_out, w_head, sessions):
    slots = incoming.shape[0]
    width = w_out.shape[0]
    classes = w_head.shape[1]
    half_rows = width * (3 * width + width + classes) // (2 * LANES)
    args = (core, incoming, labels, gain, w_project, w_out, w_head)
    vmem = pl.BlockSpec(memory_space=pltpu.VMEM)
    half = jax.ShapeDtypeStruct((half_rows, LANES), bf16)
    return pl.pallas_call(
        session_kernel,
        in_specs=[pl.BlockSpec(memory_space=pltpu.SMEM)] + [vmem] * (len(args) - 1),
        out_specs=[vmem] * 5,
        out_shape=[
            jax.ShapeDtypeStruct((sessions, classes), f32),
            jax.ShapeDtypeStruct((slots, width), bf16),
            half,
            half,
            jax.ShapeDtypeStruct((16, LANES), f32),
        ],
        scratch_shapes=[
            pltpu.VMEM((slots, 3 * width), bf16),
            pltpu.VMEM((slots, width), bf16),
            pltpu.VMEM((HEADS, slots, slots), f32),
            pltpu.VMEM((slots, 3 * width), bf16),
            pltpu.VMEM((2, half_rows, LANES), bf16),
        ],
        compiler_params=pltpu.CompilerParams(vmem_limit_bytes=VMEM_LIMIT),
        cost_estimate=cost(1e10, 5e6),
        name="session_layer",
    )(*args)


def add_by_value(codes_ref, dconv_ref, table_ref, w_rows, table_grad_ref):
    packets = codes_ref.shape[2]
    vocab = table_ref.shape[1]
    values = small_iota((vocab, packets), 0)
    codes = codes_ref[0]
    chosen = [onehot(codes[w : w + 1, :], values) for w in range(codes_ref.shape[1])]
    by_value = dot_nn(jnp.concatenate(chosen, axis=1), dconv_ref[...]).astype(bf16)
    table_grad_ref[...] += dot_nt(w_rows, by_value)
    return dot_nn(table_ref[...], by_value).astype(bf16)


def conv_back_kernel(
    capacity,
    core_ref,
    ret_ref,
    owner_ref,
    codes_ref,
    slope_ref,
    table_ref,
    w_ref,
    gain_grad_ref,
    keep_ref,
    send_ref,
    dconv_ref,
    held_ref,
    rows_ref,
    table_grad_ref,
    halves_ref,
    sem_ref,
):
    j = pl.program_id(0)
    slots, width = ret_ref.shape
    packets = owner_ref.shape[1]
    chan, vocab = table_ref.shape
    window = w_ref.shape[0]
    piece = slope_ref.shape[0] // SLOPE_PIECES

    @pl.when(j == 0)
    def _():
        copies = []
        for i in range(SLOPE_PIECES):
            at = pl.ds(i * piece, piece)
            copies.append(pltpu.make_async_copy(slope_ref.at[at, :], held_ref.at[at, :], sem_ref.at[i]))
            copies[i].start()
        own_row = owner_ref[...]
        own_col = column(own_row)
        same = (own_col == own_row) & (iota((packets, packets), 1) < iota((packets, packets), 0))
        rank = jnp.sum(jnp.where(same, 1.0, 0.0), axis=1, keepdims=True).astype(jnp.int32)
        place = flag(iota((packets, slots), 1) == own_col * capacity + rank)
        demb = dot_nn(place, ret_ref[...])
        halves_ref[...] = jnp.zeros_like(halves_ref)
        table_grad_ref[...] = jnp.zeros_like(table_grad_ref)
        for i in range(SLOPE_PIECES):
            copies[i].wait()
            for first in range(i * piece, (i + 1) * piece, packets):
                at = slice(first, first + packets)
                dconv_ref[at, :] = (demb * held_ref[at, :].astype(f32)).astype(bf16)

    at = pl.ds(pl.multiple_of(j * chan, chan), chan)
    rows_ref[at, :] = add_by_value(codes_ref, dconv_ref, table_ref, w_ref[at, :], table_grad_ref)

    @pl.when(j == pl.num_programs(0) - 1)
    def _():
        wide = width // (2 * LANES)
        for half in range(2):
            for s in range(wide):
                slab = half * wide + s
                halves_ref[half, s * window : (s + 1) * window, :] = rows_ref[:, slab * LANES : (slab + 1) * LANES]
            end = wide * window
            table_part = table_grad_ref[:, half * vocab // 2 : (half + 1) * vocab // 2]
            halves_ref[half, end : end + chan, :] = table_part.astype(bf16)
        halves_ref[0, end + chan : end + chan + 16, :] = gain_grad_ref[...].astype(bf16)
        share_out(core_ref, halves_ref, keep_ref, send_ref)


def whole(a):
    return pl.BlockSpec(a.shape, lambda j: (0,) * len(a.shape))


def conv_back(core, returned, owner, codes, slope, table_t, w_conv, gain_grad, capacity, half_rows):
    args = (returned, owner, codes, slope, table_t, w_conv, gain_grad)
    specs = [whole(a) if a.ndim == 2 else pl.BlockSpec((1, *a.shape[1:]), lambda j: (j, 0, 0)) for a in args]
    specs[3] = pl.BlockSpec(memory_space=pl.ANY)
    half = jax.ShapeDtypeStruct((half_rows, LANES), bf16)
    return pl.pallas_call(
        functools.partial(conv_back_kernel, capacity),
        grid=(KERNEL,),
        in_specs=[pl.BlockSpec(memory_space=pltpu.SMEM), *specs],
        out_specs=[whole(half), whole(half)],
        out_shape=[half, half],
        scratch_shapes=[
            pltpu.VMEM(slope.shape, bf16),
            pltpu.VMEM(slope.shape, bf16),
            pltpu.VMEM(w_conv.shape, bf16),
            pltpu.VMEM(table_t.shape, f32),
            pltpu.VMEM((2, half_rows, LANES), bf16),
            pltpu.SemaphoreType.DMA((SLOPE_PIECES,)),
        ],
        compiler_params=pltpu.CompilerParams(vmem_limit_bytes=28 * 2**20),
        cost_estimate=cost(1e9, 1e6),
        name="conv_back",
    )(core, *args)


def put_together(place_ref, piece_refs, halves_ref):
    mine, k = place_ref[0], place_ref[1]
    count = 4
    rows = halves_ref.shape[1] // count
    for d in range(count):
        at = pl.multiple_of((k ^ d) * rows, 16)
        if len(piece_refs) == count:
            own, other = piece_refs[d][0:rows, :], piece_refs[d][rows : 2 * rows, :]
        else:
            own, other = piece_refs[d][...], piece_refs[count + d][...]
        halves_ref[mine, pl.ds(at, rows), :] = own
        halves_ref[1 - mine, pl.ds(at, rows), :] = other


def early_out_kernel(place_ref, *refs):
    *pieces, project_ref, out_ref, head_ref, halves_ref = refs
    put_together(place_ref, pieces, halves_ref)
    for half in range(2):
        at = 0
        for ref in (project_ref, out_ref):
            rows, side = ref.shape[0], ref.shape[1] // 2
            for s in range(side // LANES):
                lanes = half * side + s * LANES
                ref[:, lanes : lanes + LANES] = halves_ref[half, at : at + rows, :].astype(f32)
                at += rows
        rows = head_ref.shape[0] // 2
        head_ref[half * rows : (half + 1) * rows, :] = halves_ref[half, at : at + rows, :].astype(f32)


def late_out_kernel(place_ref, *refs):
    *pieces, conv_ref, table_ref, gain_ref, halves_ref = refs
    put_together(place_ref, pieces, halves_ref)
    for half in range(2):
        at = 0
        rows, side = conv_ref.shape[0], conv_ref.shape[1] // 2
        for s in range(side // LANES):
            lanes = half * side + s * LANES
            conv_ref[:, lanes : lanes + LANES] = halves_ref[half, at : at + rows, :].astype(f32)
            at += rows
        chan, vocab = table_ref.shape
        table_ref[:, half * vocab // 2 : (half + 1) * vocab // 2] = halves_ref[half, at : at + chan, :].astype(f32)
        at += chan
        if half == 0:
            gain = halves_ref[0, at : at + 16, :].astype(f32)
            for s in range(gain_ref.shape[1] // LANES):
                gain_ref[:, s * LANES : (s + 1) * LANES] = gain[s : s + 1, :]


def assemble(kernel, place, pieces, shapes, name):
    vmem = pl.BlockSpec(memory_space=pltpu.VMEM)
    rows = sum(p.shape[0] for p in pieces) // 2
    return pl.pallas_call(
        kernel,
        in_specs=[pl.BlockSpec(memory_space=pltpu.SMEM)] + [vmem] * len(pieces),
        out_specs=[vmem] * len(shapes),
        out_shape=[jax.ShapeDtypeStruct(s, f32) for s in shapes],
        scratch_shapes=[pltpu.VMEM((2, rows, LANES), bf16)],
        compiler_params=pltpu.CompilerParams(vmem_limit_bytes=VMEM_LIMIT),
        cost_estimate=cost(1e9, 5e6),
        name=name,
    )(place, *pieces)


class Levels:
    def __init__(self, n_dp, n_rep):
        self.count = n_dp * n_rep
        self.index = lax.axis_index("dp") * n_rep + lax.axis_index("rep")
        self.levels = []
        stride, left = 1, self.count
        for size in (2, *[4] * 8):
            while size > 1 and left % size:
                size //= 2
            if size > 1:
                self.levels.append((stride, size))
                stride, left = stride * size, left // size
        assert left == 1

    def place(self, level):
        stride, size = level
        return lax.rem(lax.div(self.index, stride), size)

    def swap(self, value, level, d):
        stride, size = level
        return lax.ppermute(value, AXES, [(i, i + ((i // stride % size ^ d) - i // stride % size) * stride) for i in range(self.count)])

    def scatter_sum(self, value, level, other=None):
        size = level[1]
        value = value.reshape(size, value.shape[0] // size, value.shape[1])
        mine = self.place(level)
        got = [self.swap(lax.dynamic_index_in_dim(value, mine ^ d, 0, keepdims=False), level, d) for d in range(1, size)]
        if other is not None:
            got = after(got, other)
        total = lax.dynamic_index_in_dim(value, mine, 0, keepdims=False).astype(f32)
        for g in got:
            total = total + g.astype(f32)
        return total.astype(bf16)

    def gather(self, value, level, other=None):
        size = level[1]
        mine = self.place(level)
        got = [self.swap(value, level, d) for d in range(1, size)]
        if other is not None:
            got = after(got, other)
        out = jnp.zeros((size, *value.shape), value.dtype)
        for d, g in enumerate([value, *got]):
            out = lax.dynamic_update_index_in_dim(out, g, mine ^ d, 0)
        return out.reshape(size * value.shape[0], value.shape[1])

    def exchange_sum(self, value, level, other):
        terms = [value] + after([self.swap(value, level, d) for d in range(1, level[1])], other)
        terms = [t.astype(f32) for t in terms]
        while len(terms) > 1:
            terms = [a + b for a, b in zip(terms[::2], terms[1::2], strict=True)]
        return terms[0].astype(bf16)

    def pair_sum(self, keep, send):
        return (keep.astype(f32) + self.swap(send, self.levels[0], 1).astype(f32)).astype(bf16)

    def join(self, value):
        return jnp.concatenate([value, self.swap(value, self.levels[0], 1)], axis=0)

    def joint_pieces(self, both):
        quad = self.levels[1]
        return [both] + [self.swap(both, quad, d) for d in range(1, quad[1])]

    def pieces(self, value, other):
        quad = self.levels[1]
        own = [value] + after([self.swap(value, quad, d) for d in range(1, quad[1])], other)
        return own + [self.swap(p, self.levels[0], 1) for p in own]


def after(value, other):
    return lax.optimization_barrier((value, other))[0]


def body(packet_bytes, owner_index, session_id, class_label, byte_table, w_conv, norm_gain, w_project, w_out, w_head):
    groups = lax.axis_size("dp")
    devices = Levels(groups, lax.axis_size("rep"))
    packets, length = packet_bytes.shape
    slots = 2 * packets
    capacity = slots // groups
    width = w_conv.shape[1]
    window = w_conv.shape[0]
    vocab, chan = byte_table.shape
    sessions = class_label.shape[0]
    core = devices.place(devices.levels[0]).reshape(1)
    place = jnp.stack([devices.place(level) for level in devices.levels[:2]])

    owner = owner_index.reshape(1, packets)
    table_t = byte_table.T
    outgoing, slope, codes = embed(packet_bytes, owner, session_id.reshape(1, packets), table_t, w_conv, capacity, slots)

    def exchange(rows):
        return lax.all_to_all(
            rows.reshape(groups, capacity, rows.shape[1]), "dp", split_axis=0, concat_axis=0, tiled=True
        ).reshape(rows.shape)

    logits, back, keep, send, gain_grad = session_layer(
        core,
        exchange(outgoing),
        class_label.reshape(1, sessions),
        norm_gain.reshape(1, width),
        w_project,
        w_out,
        w_head,
        sessions,
    )
    early = devices.pair_sum(keep, send)
    used = window * width // (2 * LANES) + chan * vocab // (2 * LANES) + 16
    unit = 64
    half_rows = -(-used // unit) * unit
    _, quad, *upper = devices.levels
    keep, send = conv_back(
        core, after(exchange(back), early), owner, codes, slope, table_t, w_conv, gain_grad, capacity, half_rows
    )
    early = devices.scatter_sum(early, quad, keep)
    late = devices.pair_sum(keep, send)
    for level in upper:
        early = devices.scatter_sum(early, level, late)
    late = devices.scatter_sum(late, quad, early)
    for level in upper[::-1]:
        early = devices.gather(early, level)
    for level in upper:
        late = devices.exchange_sum(late, level, early)
    late = devices.join(late)
    grad_project, grad_out, grad_head = assemble(
        early_out_kernel, place, devices.pieces(early, late), [w_project.shape, w_out.shape, w_head.shape], "early_out"
    )
    grad_conv, table_grad, gain_grad = assemble(
        late_out_kernel, after(place, grad_head), devices.joint_pieces(late), [w_conv.shape, table_t.shape, (1, width)], "late_out"
    )
    return (logits, table_grad.T, grad_conv, gain_grad.reshape(width), grad_project, grad_out, grad_head)


def solution(mesh):
    split = P(AXES)
    rows = P(AXES, None)
    in_specs = (rows, split, split, split, P(), P(), P(), P(), P(), P())
    out_specs = (rows, P(), P(), P(), P(), P(), P())
    return jax.shard_map(body, mesh=mesh, in_specs=in_specs, out_specs=out_specs, check_vma=False)
```

```python
import functools

import jax
import jax.numpy as jnp
from jax import lax
from jax.experimental import pallas as pl
from jax.experimental.pallas import tpu as pltpu
from jax.sharding import PartitionSpec as P

KERNEL = 8
HEADS = 8
NORM_EPS = 1e-06
WIN_STEP = 8
LANES = 128
VMEM_LIMIT = 28 * 2**20

f32 = jnp.float32
bf16 = jnp.bfloat16
AXES = ("dp", "rep")


def iota(shape, dim):
    return lax.broadcasted_iota(jnp.int32, shape, dim)


def dot_nn(a, b):
    return jnp.dot(a, b, preferred_element_type=f32)


def dot_nt(a, b):
    return lax.dot_general(a, b, (((1,), (1,)), ((), ())), preferred_element_type=f32)


def dot_tn(a, b):
    return lax.dot_general(a, b, (((0,), (0,)), ((), ())), preferred_element_type=f32)


def two_parts(value):
    high = value.astype(bf16)
    return high, (value - high.astype(f32)).astype(bf16)


def flag(mask):
    return jnp.where(mask, 1.0, 0.0).astype(bf16)


def onehot(codes, values):
    return jnp.where(codes == values, jnp.ones((), bf16), jnp.zeros((), bf16))


def small_iota(shape, dim):
    return iota(shape, dim).astype(f32).astype(bf16)


def spread(row, lanes):
    return jnp.broadcast_to(row.astype(f32), (lanes, row.shape[1])).T


def column(row):
    return spread(row, LANES)[:, 0:1].astype(jnp.int32)


def cost(flops, moved):
    return pl.CostEstimate(flops=int(flops), bytes_accessed=int(moved), transcendentals=0)


def slot_places(owner_ref, slots, capacity):
    own_row = owner_ref[...]
    packets = own_row.shape[1]
    ahead = (column(own_row) == own_row) & (iota((packets, packets), 0) < iota((packets, packets), 1))
    rank = jnp.sum(jnp.where(ahead, 1.0, 0.0), axis=0, keepdims=True).astype(jnp.int32)
    return flag(iota((slots, packets), 0) == own_row * capacity + rank)


def embed_kernel(
    capacity,
    bytes_ref,
    owner_ref,
    sess_ref,
    table_ref,
    w_ref,
    out_ref,
    slope_ref,
    codes_ref,
    emb_ref,
    turned_ref,
    w_turned_ref,
):
    step = pl.program_id(0)
    packets, length = bytes_ref.shape
    positions = length // KERNEL
    chan, vocab = table_ref.shape
    width = w_ref.shape[1]

    @pl.when(step == 0)
    def _():
        emb_ref[...] = jnp.zeros_like(emb_ref)
        w_turned_ref[...] = w_ref[...].astype(f32).T.astype(bf16)
        turned_ref[...] = bytes_ref[...].astype(f32).T
        for j in range(KERNEL):
            codes_ref[j] = turned_ref[pl.ds(j, positions, stride=KERNEL), :].astype(bf16)

    here = WIN_STEP * KERNEL
    codes = turned_ref[pl.ds(pl.multiple_of(step * here, here), here), :].astype(jnp.int32)
    parts = [table_ref[:, at : at + LANES].astype(f32) for at in range(0, vocab, LANES)]
    windows = []
    for w in range(WIN_STEP):
        rows = []
        for j in range(w * KERNEL, (w + 1) * KERNEL):
            code = jnp.broadcast_to(codes[j : j + 1, :], (chan, packets))
            lane = code & (LANES - 1)
            found = [jnp.take_along_axis(p, lane, axis=1, mode="promise_in_bounds") for p in parts]
            rows.append(jnp.where(code < LANES, found[0], found[1]).astype(bf16))
        windows.append(jnp.concatenate(rows, axis=0))
    conv = dot_nn(w_turned_ref[...], jnp.concatenate(windows, axis=1))
    sigma = jax.nn.sigmoid(conv)
    act = conv * sigma
    slope_ref[...] = ((sigma + act * (1.0 - sigma)) * (1.0 / positions)).astype(bf16)
    total = emb_ref[...]
    for w in range(WIN_STEP):
        total += act[:, w * packets : (w + 1) * packets]
    emb_ref[...] = total

    @pl.when(step == pl.num_programs(0) - 1)
    def _():
        emb = (emb_ref[...] * (1.0 / positions)).astype(bf16)
        place = slot_places(owner_ref, out_ref.shape[0], capacity)
        out_ref[:, :width] = dot_nt(place, emb).astype(bf16)
        label = spread(sess_ref[...] + 1, LANES).astype(bf16)
        out_ref[:, width:] = dot_nn(place, label).astype(bf16)


def embed(packet_bytes, owner, session, table_t, w_conv, capacity, slots):
    packets, length = packet_bytes.shape
    rows = WIN_STEP * packets
    steps = length // (KERNEL * WIN_STEP)
    width = w_conv.shape[1]
    whole = lambda a: pl.BlockSpec(a.shape, lambda i: (0, 0))
    args = (packet_bytes, owner, session, table_t, w_conv)
    return pl.pallas_call(
        functools.partial(embed_kernel, capacity),
        grid=(steps,),
        in_specs=[whole(a) for a in args],
        out_specs=[
            pl.BlockSpec((slots, width + LANES), lambda i: (0, 0)),
            pl.BlockSpec((width, rows), lambda i: (0, i)),
            pl.BlockSpec((KERNEL, length // KERNEL, packets), lambda i: (0, 0, 0)),
        ],
        out_shape=[
            jax.ShapeDtypeStruct((slots, width + LANES), bf16),
            jax.ShapeDtypeStruct((width, steps * rows), bf16),
            jax.ShapeDtypeStruct((KERNEL, length // KERNEL, packets), bf16),
        ],
        scratch_shapes=[
            pltpu.VMEM((width, packets), f32),
            pltpu.VMEM((length, packets), f32),
            pltpu.VMEM((width, w_conv.shape[0]), bf16),
        ],
        compiler_params=pltpu.CompilerParams(vmem_limit_bytes=2 * VMEM_LIMIT),
        cost_estimate=cost(1e10, 5e6),
        name="embed",
    )(*args)


def share_out(core_ref, halves_ref, keep_ref, send_ref):
    mine = core_ref[0]
    keep_ref[...] = halves_ref[mine]
    send_ref[...] = halves_ref[1 - mine]


def session_kernel(
    core_ref,
    inc_ref,
    label_ref,
    gain_ref,
    wp_ref,
    wo_ref,
    wh_ref,
    logits_ref,
    back_ref,
    keep_ref,
    send_ref,
    gain_grad_ref,
    proj_ref,
    att_ref,
    mix_ref,
    dproj_ref,
    halves_ref,
):
    slots = inc_ref.shape[0]
    width = wo_ref.shape[0]
    classes = wh_ref.shape[1]
    sessions = logits_ref.shape[0]
    head = width // HEADS
    scale = head**-0.5

    embedding = inc_ref[:, :width]
    x = embedding.astype(f32)
    tags = inc_ref[:, width:].astype(f32)
    tag_col = tags[:, 0:1]
    tag_row = tags.T[0:1, :]
    gain = gain_ref[...].astype(f32)
    inverse = lax.rsqrt(jnp.mean(x * x, axis=1, keepdims=True) + NORM_EPS)
    norm_in = (x * inverse * gain).astype(bf16)
    proj_ref[...] = dot_nn(norm_in, wp_ref[...]).astype(bf16)

    def part(ref, which, h):
        at = which * width + h * head
        return ref[:, at : at + head]

    same = tag_col == tag_row
    for h in range(HEADS):
        scores = dot_nt(part(proj_ref, 0, h), part(proj_ref, 1, h)) * scale
        scores = jnp.where(same, scores, -1e30)
        shifted = jnp.exp(scores - jnp.max(scores, axis=1, keepdims=True))
        mixing = shifted / jnp.sum(shifted, axis=1, keepdims=True)
        mix_ref[h] = mixing
        att_ref[:, h * head : (h + 1) * head] = dot_nn(mixing.astype(bf16), part(proj_ref, 2, h)).astype(bf16)

    is_member = tag_row == (iota((sessions, slots), 0) + 1).astype(f32)
    member = flag(is_member)
    member_t = flag(tag_col == (iota((slots, sessions), 1) + 1).astype(f32))
    counts = jnp.maximum(jnp.sum(jnp.where(is_member, 1.0, 0.0), axis=1, keepdims=True), 1.0)
    att_high, att_low = two_parts(dot_nn(member, att_ref[...]))
    out_sum = dot_nn(att_high, wo_ref[...]) + dot_nn(att_low, wo_ref[...])
    pooled_b = ((dot_nn(member, embedding) + out_sum) / counts).astype(bf16)
    logits = dot_nn(pooled_b, wh_ref[...])
    logits_ref[...] = logits
    grown = jnp.exp(logits - jnp.max(logits, axis=1, keepdims=True))
    probs = grown / jnp.sum(grown, axis=1, keepdims=True)
    target = jnp.where(column(label_ref[...])[:sessions] == iota((sessions, classes), 1), 1.0, 0.0)
    dlogits = (probs - target) * (1.0 / sessions)
    dl_high, dl_low = two_parts(dlogits)
    grad_head = dot_tn(pooled_b, dl_high) + dot_tn(pooled_b, dl_low)
    dpooled = dot_nt(dl_high, wh_ref[...]) + dot_nt(dl_low, wh_ref[...])
    dsess = dpooled / counts
    dsess_b, dsess_low = two_parts(dsess)
    dhidden = dot_nn(member_t, dsess_b) + dot_nn(member_t, dsess_low)
    grad_out = dot_tn(att_high, dsess_b) + dot_tn(att_low, dsess_b)
    datt_s = dot_nt(dsess_b, wo_ref[...]).astype(bf16)
    datt = dot_nn(member_t, datt_s).astype(bf16)

    for h in range(HEADS):
        cols = slice(h * head, (h + 1) * head)
        mixing = mix_ref[h]
        dmix_s = dot_nt(datt_s[:, cols], part(proj_ref, 2, h))
        dmixing = jnp.sum(jnp.where(is_member, dmix_s, 0.0), axis=0, keepdims=True)
        weighted = mixing * dmixing
        dscores = ((weighted - mixing * jnp.sum(weighted, axis=1, keepdims=True)) * scale).astype(bf16)
        dq = dot_nn(dscores, part(proj_ref, 1, h))
        dk = dot_tn(dscores, part(proj_ref, 0, h))
        dv = dot_tn(mixing.astype(bf16), datt[:, cols])
        for which, d in ((0, dq), (1, dk), (2, dv)):
            at = which * width + h * head
            dproj_ref[:, at : at + head] = d.astype(bf16)

    at = [0, 0]

    def put(half, block):
        for s in range(block.shape[1] // LANES):
            rows = block.shape[0]
            halves_ref[half, at[half] : at[half] + rows, :] = block[:, s * LANES : (s + 1) * LANES].astype(bf16)
            at[half] += rows

    side = 3 * width // 2
    for half in range(2):
        put(half, dot_tn(norm_in, dproj_ref[:, half * side : (half + 1) * side]))
        put(half, grad_out[:, half * width // 2 : (half + 1) * width // 2])
        put(half, grad_head[half * width // 2 : (half + 1) * width // 2, :])
    share_out(core_ref, halves_ref, keep_ref, send_ref)
    dnorm = dot_nt(dproj_ref[...], wp_ref[...])
    grad_gain = jnp.sum(dnorm * x * inverse, axis=0, keepdims=True)
    gain_grad_ref[...] = jnp.zeros_like(gain_grad_ref)
    for s in range(width // LANES):
        gain_grad_ref[s : s + 1, :] = grad_gain[:, s * LANES : (s + 1) * LANES]
    scaled = dnorm * gain
    slant = jnp.mean(x * scaled, axis=1, keepdims=True) * (inverse * inverse * inverse)
    back_ref[...] = (inverse * scaled - x * slant + dhidden).astype(bf16)


def session_layer(core, incoming, labels, gain, w_project, w_out, w_head, sessions):
    slots = incoming.shape[0]
    width = w_out.shape[0]
    classes = w_head.shape[1]
    half_rows = width * (3 * width + width + classes) // (2 * LANES)
    args = (core, incoming, labels, gain, w_project, w_out, w_head)
    vmem = pl.BlockSpec(memory_space=pltpu.VMEM)
    half = jax.ShapeDtypeStruct((half_rows, LANES), bf16)
    return pl.pallas_call(
        session_kernel,
        in_specs=[pl.BlockSpec(memory_space=pltpu.SMEM)] + [vmem] * (len(args) - 1),
        out_specs=[vmem] * 5,
        out_shape=[
            jax.ShapeDtypeStruct((sessions, classes), f32),
            jax.ShapeDtypeStruct((slots, width), bf16),
            half,
            half,
            jax.ShapeDtypeStruct((16, LANES), f32),
        ],
        scratch_shapes=[
            pltpu.VMEM((slots, 3 * width), bf16),
            pltpu.VMEM((slots, width), bf16),
            pltpu.VMEM((HEADS, slots, slots), f32),
            pltpu.VMEM((slots, 3 * width), bf16),
            pltpu.VMEM((2, half_rows, LANES), bf16),
        ],
        compiler_params=pltpu.CompilerParams(vmem_limit_bytes=VMEM_LIMIT),
        cost_estimate=cost(1e10, 5e6),
        name="session_layer",
    )(*args)


def add_by_value(codes_ref, dconv_ref, table_ref, w_rows, table_grad_ref):
    packets = codes_ref.shape[2]
    vocab = table_ref.shape[1]
    values = small_iota((vocab, packets), 0)
    codes = codes_ref[0]
    chosen = [onehot(codes[w : w + 1, :], values) for w in range(codes_ref.shape[1])]
    by_value = dot_nn(jnp.concatenate(chosen, axis=1), dconv_ref[...]).astype(bf16)
    table_grad_ref[...] += dot_nt(w_rows, by_value)
    return dot_nn(table_ref[...], by_value).astype(bf16)


def conv_back_kernel(
    capacity,
    core_ref,
    ret_ref,
    owner_ref,
    codes_ref,
    slope_ref,
    table_ref,
    w_ref,
    gain_grad_ref,
    keep_ref,
    send_ref,
    dconv_ref,
    rows_ref,
    table_grad_ref,
    halves_ref,
):
    j = pl.program_id(0)
    slots, width = ret_ref.shape
    packets = owner_ref.shape[1]
    chan, vocab = table_ref.shape
    window = w_ref.shape[0]

    @pl.when(j == 0)
    def _():
        demb = dot_tn(slot_places(owner_ref, slots, capacity), ret_ref[...])
        halves_ref[...] = jnp.zeros_like(halves_ref)
        table_grad_ref[...] = jnp.zeros_like(table_grad_ref)
        for first in range(0, slope_ref.shape[1], packets):
            at = slice(first, first + packets)
            dconv_ref[at, :] = (demb * slope_ref[:, at].astype(f32).T).astype(bf16)

    at = pl.ds(pl.multiple_of(j * chan, chan), chan)
    rows_ref[at, :] = add_by_value(codes_ref, dconv_ref, table_ref, w_ref[at, :], table_grad_ref)

    @pl.when(j == pl.num_programs(0) - 1)
    def _():
        wide = width // (2 * LANES)
        for half in range(2):
            for s in range(wide):
                slab = half * wide + s
                halves_ref[half, s * window : (s + 1) * window, :] = rows_ref[:, slab * LANES : (slab + 1) * LANES]
            end = wide * window
            table_part = table_grad_ref[:, half * vocab // 2 : (half + 1) * vocab // 2]
            halves_ref[half, end : end + chan, :] = table_part.astype(bf16)
        halves_ref[0, end + chan : end + chan + 16, :] = gain_grad_ref[...].astype(bf16)
        share_out(core_ref, halves_ref, keep_ref, send_ref)


def whole(a):
    return pl.BlockSpec(a.shape, lambda j: (0,) * len(a.shape))


def conv_back(core, returned, owner, codes, slope, table_t, w_conv, gain_grad, capacity, half_rows):
    args = (returned, owner, codes, slope, table_t, w_conv, gain_grad)
    specs = [whole(a) if a.ndim == 2 else pl.BlockSpec((1, *a.shape[1:]), lambda j: (j, 0, 0)) for a in args]
    half = jax.ShapeDtypeStruct((half_rows, LANES), bf16)
    return pl.pallas_call(
        functools.partial(conv_back_kernel, capacity),
        grid=(KERNEL,),
        in_specs=[pl.BlockSpec(memory_space=pltpu.SMEM), *specs],
        out_specs=[whole(half), whole(half)],
        out_shape=[half, half],
        scratch_shapes=[
            pltpu.VMEM(slope.shape[::-1], bf16),
            pltpu.VMEM(w_conv.shape, bf16),
            pltpu.VMEM(table_t.shape, f32),
            pltpu.VMEM((2, half_rows, LANES), bf16),
        ],
        compiler_params=pltpu.CompilerParams(vmem_limit_bytes=28 * 2**20),
        cost_estimate=cost(1e9, 1e6),
        name="conv_back",
    )(core, *args)


def put_together(place_ref, piece_refs, halves_ref):
    mine, k = place_ref[0], place_ref[1]
    count = 4
    rows = halves_ref.shape[1] // count
    for d in range(count):
        at = pl.multiple_of((k ^ d) * rows, 16)
        if len(piece_refs) == count:
            own, other = piece_refs[d][0:rows, :], piece_refs[d][rows : 2 * rows, :]
        else:
            own, other = piece_refs[d][...], piece_refs[count + d][...]
        halves_ref[mine, pl.ds(at, rows), :] = own
        halves_ref[1 - mine, pl.ds(at, rows), :] = other


def early_out_kernel(place_ref, *refs):
    *pieces, project_ref, out_ref, head_ref, halves_ref = refs
    put_together(place_ref, pieces, halves_ref)
    for half in range(2):
        at = 0
        for ref in (project_ref, out_ref):
            rows, side = ref.shape[0], ref.shape[1] // 2
            for s in range(side // LANES):
                lanes = half * side + s * LANES
                ref[:, lanes : lanes + LANES] = halves_ref[half, at : at + rows, :].astype(f32)
                at += rows
        rows = head_ref.shape[0] // 2
        head_ref[half * rows : (half + 1) * rows, :] = halves_ref[half, at : at + rows, :].astype(f32)


def late_out_kernel(place_ref, *refs):
    *pieces, conv_ref, table_ref, gain_ref, halves_ref = refs
    put_together(place_ref, pieces, halves_ref)
    for half in range(2):
        at = 0
        rows, side = conv_ref.shape[0], conv_ref.shape[1] // 2
        for s in range(side // LANES):
            lanes = half * side + s * LANES
            conv_ref[:, lanes : lanes + LANES] = halves_ref[half, at : at + rows, :].astype(f32)
            at += rows
        chan, vocab = table_ref.shape
        table_ref[:, half * vocab // 2 : (half + 1) * vocab // 2] = halves_ref[half, at : at + chan, :].astype(f32)
        at += chan
        if half == 0:
            gain = halves_ref[0, at : at + 16, :].astype(f32)
            for s in range(gain_ref.shape[1] // LANES):
                gain_ref[:, s * LANES : (s + 1) * LANES] = gain[s : s + 1, :]


def assemble(kernel, place, pieces, shapes, name):
    vmem = pl.BlockSpec(memory_space=pltpu.VMEM)
    rows = sum(p.shape[0] for p in pieces) // 2
    return pl.pallas_call(
        kernel,
        in_specs=[pl.BlockSpec(memory_space=pltpu.SMEM)] + [vmem] * len(pieces),
        out_specs=[vmem] * len(shapes),
        out_shape=[jax.ShapeDtypeStruct(s, f32) for s in shapes],
        scratch_shapes=[pltpu.VMEM((2, rows, LANES), bf16)],
        compiler_params=pltpu.CompilerParams(vmem_limit_bytes=VMEM_LIMIT),
        cost_estimate=cost(1e9, 5e6),
        name=name,
    )(place, *pieces)


class Levels:
    def __init__(self, n_dp, n_rep):
        self.count = n_dp * n_rep
        self.index = lax.axis_index("dp") * n_rep + lax.axis_index("rep")
        self.levels = []
        stride, left = 1, self.count
        for size in (2, *[4] * 8):
            while size > 1 and left % size:
                size //= 2
            if size > 1:
                self.levels.append((stride, size))
                stride, left = stride * size, left // size
        assert left == 1

    def place(self, level):
        stride, size = level
        return lax.rem(lax.div(self.index, stride), size)

    def swap(self, value, level, d):
        stride, size = level
        return lax.ppermute(value, AXES, [(i, i + ((i // stride % size ^ d) - i // stride % size) * stride) for i in range(self.count)])

    def scatter_sum(self, value, level, other=None):
        size = level[1]
        value = value.reshape(size, value.shape[0] // size, value.shape[1])
        mine = self.place(level)
        got = [self.swap(lax.dynamic_index_in_dim(value, mine ^ d, 0, keepdims=False), level, d) for d in range(1, size)]
        if other is not None:
            got = after(got, other)
        total = lax.dynamic_index_in_dim(value, mine, 0, keepdims=False).astype(f32)
        for g in got:
            total = total + g.astype(f32)
        return total.astype(bf16)

    def gather(self, value, level, other=None):
        size = level[1]
        mine = self.place(level)
        got = [self.swap(value, level, d) for d in range(1, size)]
        if other is not None:
            got = after(got, other)
        out = jnp.zeros((size, *value.shape), value.dtype)
        for d, g in enumerate([value, *got]):
            out = lax.dynamic_update_index_in_dim(out, g, mine ^ d, 0)
        return out.reshape(size * value.shape[0], value.shape[1])

    def exchange_sum(self, value, level, other):
        terms = [value] + after([self.swap(value, level, d) for d in range(1, level[1])], other)
        terms = [t.astype(f32) for t in terms]
        while len(terms) > 1:
            terms = [a + b for a, b in zip(terms[::2], terms[1::2], strict=True)]
        return terms[0].astype(bf16)

    def pair_sum(self, keep, send):
        return (keep.astype(f32) + self.swap(send, self.levels[0], 1).astype(f32)).astype(bf16)

    def join(self, value):
        return jnp.concatenate([value, self.swap(value, self.levels[0], 1)], axis=0)

    def joint_pieces(self, both):
        quad = self.levels[1]
        return [both] + [self.swap(both, quad, d) for d in range(1, quad[1])]

    def pieces(self, value, other):
        quad = self.levels[1]
        own = [value] + after([self.swap(value, quad, d) for d in range(1, quad[1])], other)
        return own + [self.swap(p, self.levels[0], 1) for p in own]


def after(value, other):
    return lax.optimization_barrier((value, other))[0]


def body(packet_bytes, owner_index, session_id, class_label, byte_table, w_conv, norm_gain, w_project, w_out, w_head):
    groups = lax.axis_size("dp")
    devices = Levels(groups, lax.axis_size("rep"))
    packets, length = packet_bytes.shape
    slots = 2 * packets
    capacity = slots // groups
    width = w_conv.shape[1]
    window = w_conv.shape[0]
    vocab, chan = byte_table.shape
    sessions = class_label.shape[0]
    core = devices.place(devices.levels[0]).reshape(1)
    place = jnp.stack([devices.place(level) for level in devices.levels[:2]])

    owner = owner_index.reshape(1, packets)
    table_t = byte_table.T
    outgoing, slope, codes = embed(packet_bytes, owner, session_id.reshape(1, packets), table_t, w_conv, capacity, slots)

    def exchange(rows):
        return lax.all_to_all(
            rows.reshape(groups, capacity, rows.shape[1]), "dp", split_axis=0, concat_axis=0, tiled=True
        ).reshape(rows.shape)

    logits, back, keep, send, gain_grad = session_layer(
        core,
        exchange(outgoing),
        class_label.reshape(1, sessions),
        norm_gain.reshape(1, width),
        w_project,
        w_out,
        w_head,
        sessions,
    )
    early = devices.pair_sum(keep, send)
    used = window * width // (2 * LANES) + chan * vocab // (2 * LANES) + 16
    unit = 64
    half_rows = -(-used // unit) * unit
    _, quad, *upper = devices.levels
    keep, send = conv_back(
        core, after(exchange(back), early), owner, codes, slope, table_t, w_conv, gain_grad, capacity, half_rows
    )
    early = devices.scatter_sum(early, quad, keep)
    late = devices.pair_sum(keep, send)
    for level in upper:
        early = devices.scatter_sum(early, level, late)
    late = devices.scatter_sum(late, quad, early)
    for level in upper[::-1]:
        early = devices.gather(early, level)
    for level in upper:
        late = devices.exchange_sum(late, level, early)
    late = devices.join(late)
    grad_project, grad_out, grad_head = assemble(
        early_out_kernel, place, devices.pieces(early, late), [w_project.shape, w_out.shape, w_head.shape], "early_out"
    )
    grad_conv, table_grad, gain_grad = assemble(
        late_out_kernel, after(place, grad_head), devices.joint_pieces(late), [w_conv.shape, table_t.shape, (1, width)], "late_out"
    )
    return (logits, table_grad.T, grad_conv, gain_grad.reshape(width), grad_project, grad_out, grad_head)


def solution(mesh):
    split = P(AXES)
    rows = P(AXES, None)
    in_specs = (rows, split, split, split, P(), P(), P(), P(), P(), P())
    out_specs = (rows, P(), P(), P(), P(), P(), P())
    return jax.shard_map(body, mesh=mesh, in_specs=in_specs, out_specs=out_specs, check_vma=False)
```

```python
import functools

import jax
import jax.numpy as jnp
from jax import lax
from jax.experimental import pallas as pl
from jax.experimental.pallas import tpu as pltpu
from jax.sharding import PartitionSpec as P

KERNEL = 8
HEADS = 8
NORM_EPS = 1e-06
WIN_STEP = 8
BYTE_STEP = 4
LANES = 128
VMEM_LIMIT = 28 * 2**20

f32 = jnp.float32
bf16 = jnp.bfloat16
AXES = ("dp", "rep")


def iota(shape, dim):
    return lax.broadcasted_iota(jnp.int32, shape, dim)


def dot_nn(a, b):
    return jnp.dot(a, b, preferred_element_type=f32)


def dot_nt(a, b):
    return lax.dot_general(a, b, (((1,), (1,)), ((), ())), preferred_element_type=f32)


def dot_tn(a, b):
    return lax.dot_general(a, b, (((0,), (0,)), ((), ())), preferred_element_type=f32)


def two_parts(value):
    high = value.astype(bf16)
    return high, (value - high.astype(f32)).astype(bf16)


def flag(mask):
    return jnp.where(mask, 1.0, 0.0).astype(bf16)


def onehot(codes, values):
    return jnp.where(codes == values, jnp.ones((), bf16), jnp.zeros((), bf16))


def small_iota(shape, dim):
    return iota(shape, dim).astype(f32).astype(bf16)


def spread(row, lanes):
    return jnp.broadcast_to(row.astype(f32), (lanes, row.shape[1])).T


def column(row):
    return spread(row, LANES)[:, 0:1].astype(jnp.int32)


def cost(flops, moved):
    return pl.CostEstimate(flops=int(flops), bytes_accessed=int(moved), transcendentals=0)


def slot_places(owner_ref, slots, capacity):
    own_row = owner_ref[...]
    packets = own_row.shape[1]
    ahead = (column(own_row) == own_row) & (iota((packets, packets), 0) < iota((packets, packets), 1))
    rank = jnp.sum(jnp.where(ahead, 1.0, 0.0), axis=0, keepdims=True).astype(jnp.int32)
    return flag(iota((slots, packets), 0) == own_row * capacity + rank)


def embed_kernel(
    capacity,
    bytes_ref,
    owner_ref,
    sess_ref,
    table_ref,
    w_ref,
    out_ref,
    slope_ref,
    codes_ref,
    emb_ref,
    turned_ref,
    w_turned_ref,
):
    step = pl.program_id(0)
    packets, length = bytes_ref.shape
    positions = length // KERNEL
    chan, vocab = table_ref.shape
    width = w_ref.shape[1]

    @pl.when(step == 0)
    def _():
        emb_ref[...] = jnp.zeros_like(emb_ref)
        w_turned_ref[...] = w_ref[...].astype(f32).T.astype(bf16)
        turned_ref[...] = bytes_ref[...].astype(f32).T
        for j in range(KERNEL):
            codes_ref[j] = turned_ref[pl.ds(j, positions, stride=KERNEL), :].astype(bf16)

    here = WIN_STEP * KERNEL
    codes = turned_ref[pl.ds(pl.multiple_of(step * here, here), here), :].astype(jnp.int32)
    parts = [table_ref[:, at : at + LANES].astype(f32) for at in range(0, vocab, LANES)]
    windows = []
    for w in range(WIN_STEP):
        rows = []
        for j in range(w * KERNEL, (w + 1) * KERNEL):
            code = jnp.broadcast_to(codes[j : j + 1, :], (chan, packets))
            lane = code & (LANES - 1)
            found = [jnp.take_along_axis(p, lane, axis=1, mode="promise_in_bounds") for p in parts]
            rows.append(jnp.where(code < LANES, found[0], found[1]).astype(bf16))
        windows.append(jnp.concatenate(rows, axis=0))
    conv = dot_nn(w_turned_ref[...], jnp.concatenate(windows, axis=1))
    sigma = jax.nn.sigmoid(conv)
    act = conv * sigma
    slope_ref[...] = ((sigma + act * (1.0 - sigma)) * (1.0 / positions)).astype(bf16)
    total = emb_ref[...]
    for w in range(WIN_STEP):
        total += act[:, w * packets : (w + 1) * packets]
    emb_ref[...] = total

    @pl.when(step == pl.num_programs(0) - 1)
    def _():
        emb = (emb_ref[...] * (1.0 / positions)).astype(bf16)
        place = slot_places(owner_ref, out_ref.shape[0], capacity)
        out_ref[:, :width] = dot_nt(place, emb).astype(bf16)
        label = spread(sess_ref[...] + 1, LANES).astype(bf16)
        out_ref[:, width:] = dot_nn(place, label).astype(bf16)


def embed(packet_bytes, owner, session, table_t, w_conv, capacity, slots):
    packets, length = packet_bytes.shape
    rows = WIN_STEP * packets
    steps = length // (KERNEL * WIN_STEP)
    width = w_conv.shape[1]
    whole = lambda a: pl.BlockSpec(a.shape, lambda i: (0, 0))
    args = (packet_bytes, owner, session, table_t, w_conv)
    return pl.pallas_call(
        functools.partial(embed_kernel, capacity),
        grid=(steps,),
        in_specs=[whole(a) for a in args],
        out_specs=[
            pl.BlockSpec((slots, width + LANES), lambda i: (0, 0)),
            pl.BlockSpec((width, rows), lambda i: (0, i)),
            pl.BlockSpec((KERNEL, length // KERNEL, packets), lambda i: (0, 0, 0)),
        ],
        out_shape=[
            jax.ShapeDtypeStruct((slots, width + LANES), bf16),
            jax.ShapeDtypeStruct((width, steps * rows), bf16),
            jax.ShapeDtypeStruct((KERNEL, length // KERNEL, packets), bf16),
        ],
        scratch_shapes=[
            pltpu.VMEM((width, packets), f32),
            pltpu.VMEM((length, packets), f32),
            pltpu.VMEM((width, w_conv.shape[0]), bf16),
        ],
        compiler_params=pltpu.CompilerParams(vmem_limit_bytes=2 * VMEM_LIMIT),
        cost_estimate=cost(1e10, 5e6),
        name="embed",
    )(*args)


def share_out(place_ref, halves_ref, keep_ref, send_ref):
    mine, k = place_ref[0] & 1, place_ref[0] >> 1
    rows = keep_ref.shape[0] // 4
    for d in range(4):
        at = pl.ds(pl.multiple_of((k ^ d) * rows, 16), rows)
        keep_ref[d * rows : (d + 1) * rows, :] = halves_ref[mine, at, :]
        send_ref[d * rows : (d + 1) * rows, :] = halves_ref[1 - mine, at, :]


def session_kernel(
    core_ref,
    inc_ref,
    label_ref,
    gain_ref,
    wp_ref,
    wo_ref,
    wh_ref,
    logits_ref,
    back_ref,
    keep_ref,
    send_ref,
    gain_grad_ref,
    proj_ref,
    att_ref,
    mix_ref,
    dproj_ref,
    halves_ref,
):
    slots = inc_ref.shape[0]
    width = wo_ref.shape[0]
    classes = wh_ref.shape[1]
    sessions = logits_ref.shape[0]
    head = width // HEADS
    scale = head**-0.5

    embedding = inc_ref[:, :width]
    x = embedding.astype(f32)
    tags = inc_ref[:, width:].astype(f32)
    tag_col = tags[:, 0:1]
    tag_row = tags.T[0:1, :]
    gain = gain_ref[...].astype(f32)
    inverse = lax.rsqrt(jnp.mean(x * x, axis=1, keepdims=True) + NORM_EPS)
    norm_in = (x * inverse * gain).astype(bf16)
    proj_ref[...] = dot_nn(norm_in, wp_ref[...]).astype(bf16)

    def part(ref, which, h):
        at = which * width + h * head
        return ref[:, at : at + head]

    same = tag_col == tag_row
    for h in range(HEADS):
        scores = dot_nt(part(proj_ref, 0, h), part(proj_ref, 1, h)) * scale
        scores = jnp.where(same, scores, -1e30)
        shifted = jnp.exp(scores - jnp.max(scores, axis=1, keepdims=True))
        mixing = shifted / jnp.sum(shifted, axis=1, keepdims=True)
        mix_ref[h] = mixing
        att_ref[:, h * head : (h + 1) * head] = dot_nn(mixing.astype(bf16), part(proj_ref, 2, h)).astype(bf16)

    is_member = tag_row == (iota((sessions, slots), 0) + 1).astype(f32)
    member = flag(is_member)
    member_t = flag(tag_col == (iota((slots, sessions), 1) + 1).astype(f32))
    counts = jnp.maximum(jnp.sum(jnp.where(is_member, 1.0, 0.0), axis=1, keepdims=True), 1.0)
    att_high, att_low = two_parts(dot_nn(member, att_ref[...]))
    out_sum = dot_nn(att_high, wo_ref[...]) + dot_nn(att_low, wo_ref[...])
    pooled_b = ((dot_nn(member, embedding) + out_sum) / counts).astype(bf16)
    logits = dot_nn(pooled_b, wh_ref[...])
    logits_ref[...] = logits
    grown = jnp.exp(logits - jnp.max(logits, axis=1, keepdims=True))
    probs = grown / jnp.sum(grown, axis=1, keepdims=True)
    target = jnp.where(column(label_ref[...])[:sessions] == iota((sessions, classes), 1), 1.0, 0.0)
    dlogits = (probs - target) * (1.0 / sessions)
    dl_high, dl_low = two_parts(dlogits)
    grad_head = dot_tn(pooled_b, dl_high) + dot_tn(pooled_b, dl_low)
    dpooled = dot_nt(dl_high, wh_ref[...]) + dot_nt(dl_low, wh_ref[...])
    dsess = dpooled / counts
    dsess_b, dsess_low = two_parts(dsess)
    dhidden = dot_nn(member_t, dsess_b) + dot_nn(member_t, dsess_low)
    grad_out = dot_tn(att_high, dsess_b) + dot_tn(att_low, dsess_b)
    datt_s = dot_nt(dsess_b, wo_ref[...]).astype(bf16)
    datt = dot_nn(member_t, datt_s).astype(bf16)

    for h in range(HEADS):
        cols = slice(h * head, (h + 1) * head)
        mixing = mix_ref[h]
        dmix_s = dot_nt(datt_s[:, cols], part(proj_ref, 2, h))
        dmixing = jnp.sum(jnp.where(is_member, dmix_s, 0.0), axis=0, keepdims=True)
        weighted = mixing * dmixing
        dscores = ((weighted - mixing * jnp.sum(weighted, axis=1, keepdims=True)) * scale).astype(bf16)
        dq = dot_nn(dscores, part(proj_ref, 1, h))
        dk = dot_tn(dscores, part(proj_ref, 0, h))
        dv = dot_tn(mixing.astype(bf16), datt[:, cols])
        for which, d in ((0, dq), (1, dk), (2, dv)):
            at = which * width + h * head
            dproj_ref[:, at : at + head] = d.astype(bf16)

    at = [0, 0]

    def put(half, block):
        for s in range(block.shape[1] // LANES):
            rows = block.shape[0]
            halves_ref[half, at[half] : at[half] + rows, :] = block[:, s * LANES : (s + 1) * LANES].astype(bf16)
            at[half] += rows

    side = 3 * width // 2
    for half in range(2):
        put(half, dot_tn(norm_in, dproj_ref[:, half * side : (half + 1) * side]))
        put(half, grad_out[:, half * width // 2 : (half + 1) * width // 2])
        put(half, grad_head[half * width // 2 : (half + 1) * width // 2, :])
    share_out(core_ref, halves_ref, keep_ref, send_ref)
    dnorm = dot_nt(dproj_ref[...], wp_ref[...])
    grad_gain = jnp.sum(dnorm * x * inverse, axis=0, keepdims=True)
    gain_grad_ref[...] = jnp.zeros_like(gain_grad_ref)
    for s in range(width // LANES):
        gain_grad_ref[s : s + 1, :] = grad_gain[:, s * LANES : (s + 1) * LANES]
    scaled = dnorm * gain
    slant = jnp.mean(x * scaled, axis=1, keepdims=True) * (inverse * inverse * inverse)
    back_ref[...] = (inverse * scaled - x * slant + dhidden).astype(bf16)


def session_layer(core, incoming, labels, gain, w_project, w_out, w_head, sessions):
    slots = incoming.shape[0]
    width = w_out.shape[0]
    classes = w_head.shape[1]
    half_rows = width * (3 * width + width + classes) // (2 * LANES)
    args = (core, incoming, labels, gain, w_project, w_out, w_head)
    vmem = pl.BlockSpec(memory_space=pltpu.VMEM)
    half = jax.ShapeDtypeStruct((half_rows, LANES), bf16)
    return pl.pallas_call(
        session_kernel,
        in_specs=[pl.BlockSpec(memory_space=pltpu.SMEM)] + [vmem] * (len(args) - 1),
        out_specs=[vmem] * 5,
        out_shape=[
            jax.ShapeDtypeStruct((sessions, classes), f32),
            jax.ShapeDtypeStruct((slots, width), bf16),
            half,
            half,
            jax.ShapeDtypeStruct((16, LANES), f32),
        ],
        scratch_shapes=[
            pltpu.VMEM((slots, 3 * width), bf16),
            pltpu.VMEM((slots, width), bf16),
            pltpu.VMEM((HEADS, slots, slots), f32),
            pltpu.VMEM((slots, 3 * width), bf16),
            pltpu.VMEM((2, half_rows, LANES), bf16),
        ],
        compiler_params=pltpu.CompilerParams(vmem_limit_bytes=VMEM_LIMIT),
        cost_estimate=cost(1e10, 5e6),
        name="session_layer",
    )(*args)


def add_by_value(codes_ref, dconv_ref, table_ref, w_ref, rows_ref, table_grad_ref, step):
    places, positions, packets = codes_ref.shape
    chan, vocab = table_ref.shape
    values = small_iota((vocab, packets), 0)
    blocks = []
    for i in range(places):
        codes = codes_ref[i]
        blocks.append(jnp.concatenate([onehot(codes[w : w + 1, :], values) for w in range(positions)], axis=1))
    sums = dot_nn(jnp.concatenate(blocks, axis=0), dconv_ref[...]).astype(bf16)
    for i in range(places):
        by_value = sums[i * vocab : (i + 1) * vocab]
        at = pl.ds(pl.multiple_of((step * places + i) * chan, chan), chan)
        table_grad_ref[...] += dot_nt(w_ref[at, :], by_value)
        rows_ref[at, :] = dot_nn(table_ref[...], by_value).astype(bf16)


def conv_back_kernel(
    capacity,
    core_ref,
    ret_ref,
    owner_ref,
    codes_ref,
    slope_ref,
    table_ref,
    w_ref,
    gain_grad_ref,
    keep_ref,
    send_ref,
    dconv_ref,
    rows_ref,
    table_grad_ref,
    halves_ref,
):
    j = pl.program_id(0)
    slots, width = ret_ref.shape
    packets = owner_ref.shape[1]
    chan, vocab = table_ref.shape
    window = w_ref.shape[0]

    @pl.when(j == 0)
    def _():
        demb = dot_tn(slot_places(owner_ref, slots, capacity), ret_ref[...])
        halves_ref[...] = jnp.zeros_like(halves_ref)
        table_grad_ref[...] = jnp.zeros_like(table_grad_ref)
        for first in range(0, slope_ref.shape[1], packets):
            at = slice(first, first + packets)
            dconv_ref[at, :] = (demb * slope_ref[:, at].astype(f32).T).astype(bf16)

    add_by_value(codes_ref, dconv_ref, table_ref, w_ref, rows_ref, table_grad_ref, j)

    @pl.when(j == pl.num_programs(0) - 1)
    def _():
        wide = width // (2 * LANES)
        for half in range(2):
            for s in range(wide):
                slab = half * wide + s
                halves_ref[half, s * window : (s + 1) * window, :] = rows_ref[:, slab * LANES : (slab + 1) * LANES]
            end = wide * window
            table_part = table_grad_ref[:, half * vocab // 2 : (half + 1) * vocab // 2]
            halves_ref[half, end : end + chan, :] = table_part.astype(bf16)
        halves_ref[0, end + chan : end + chan + 16, :] = gain_grad_ref[...].astype(bf16)
        share_out(core_ref, halves_ref, keep_ref, send_ref)


def whole(a):
    return pl.BlockSpec(a.shape, lambda j: (0,) * len(a.shape))


def conv_back(core, returned, owner, codes, slope, table_t, w_conv, gain_grad, capacity, half_rows):
    args = (returned, owner, codes, slope, table_t, w_conv, gain_grad)
    specs = [whole(a) if a.ndim == 2 else pl.BlockSpec((BYTE_STEP, *a.shape[1:]), lambda j: (j, 0, 0)) for a in args]
    half = jax.ShapeDtypeStruct((half_rows, LANES), bf16)
    return pl.pallas_call(
        functools.partial(conv_back_kernel, capacity),
        grid=(KERNEL // BYTE_STEP,),
        in_specs=[pl.BlockSpec(memory_space=pltpu.SMEM), *specs],
        out_specs=[whole(half), whole(half)],
        out_shape=[half, half],
        scratch_shapes=[
            pltpu.VMEM(slope.shape[::-1], bf16),
            pltpu.VMEM(w_conv.shape, bf16),
            pltpu.VMEM(table_t.shape, f32),
            pltpu.VMEM((2, half_rows, LANES), bf16),
        ],
        compiler_params=pltpu.CompilerParams(vmem_limit_bytes=28 * 2**20),
        cost_estimate=cost(1e9, 1e6),
        name="conv_back",
    )(core, *args)


def put_together(place_ref, piece_refs, halves_ref):
    mine, k = place_ref[0] & 1, place_ref[0] >> 1
    count = 4
    rows = halves_ref.shape[1] // count
    for d in range(count):
        at = pl.multiple_of((k ^ d) * rows, 16)
        if len(piece_refs) == count:
            own, other = piece_refs[d][0:rows, :], piece_refs[d][rows : 2 * rows, :]
        else:
            own, other = piece_refs[d][...], piece_refs[count + d][...]
        halves_ref[mine, pl.ds(at, rows), :] = own
        halves_ref[1 - mine, pl.ds(at, rows), :] = other


def early_out_kernel(place_ref, *refs):
    *pieces, project_ref, out_ref, head_ref, halves_ref = refs
    put_together(place_ref, pieces, halves_ref)
    for half in range(2):
        at = 0
        for ref in (project_ref, out_ref):
            rows, side = ref.shape[0], ref.shape[1] // 2
            for s in range(side // LANES):
                lanes = half * side + s * LANES
                ref[:, lanes : lanes + LANES] = halves_ref[half, at : at + rows, :].astype(f32)
                at += rows
        rows = head_ref.shape[0] // 2
        head_ref[half * rows : (half + 1) * rows, :] = halves_ref[half, at : at + rows, :].astype(f32)


def late_out_kernel(place_ref, *refs):
    *pieces, conv_ref, table_ref, gain_ref, halves_ref = refs
    put_together(place_ref, pieces, halves_ref)
    for half in range(2):
        at = 0
        rows, side = conv_ref.shape[0], conv_ref.shape[1] // 2
        for s in range(side // LANES):
            lanes = half * side + s * LANES
            conv_ref[:, lanes : lanes + LANES] = halves_ref[half, at : at + rows, :].astype(f32)
            at += rows
        chan, vocab = table_ref.shape
        table_ref[:, half * vocab // 2 : (half + 1) * vocab // 2] = halves_ref[half, at : at + chan, :].astype(f32)
        at += chan
        if half == 0:
            gain = halves_ref[0, at : at + 16, :].astype(f32)
            for s in range(gain_ref.shape[1] // LANES):
                gain_ref[:, s * LANES : (s + 1) * LANES] = gain[s : s + 1, :]


def assemble(kernel, place, pieces, shapes, name):
    vmem = pl.BlockSpec(memory_space=pltpu.VMEM)
    rows = sum(p.shape[0] for p in pieces) // 2
    return pl.pallas_call(
        kernel,
        in_specs=[pl.BlockSpec(memory_space=pltpu.SMEM)] + [vmem] * len(pieces),
        out_specs=[vmem] * len(shapes),
        out_shape=[jax.ShapeDtypeStruct(s, f32) for s in shapes],
        scratch_shapes=[pltpu.VMEM((2, rows, LANES), bf16)],
        compiler_params=pltpu.CompilerParams(vmem_limit_bytes=VMEM_LIMIT),
        cost_estimate=cost(1e9, 5e6),
        name=name,
    )(place, *pieces)


class Levels:
    def __init__(self, n_dp, n_rep):
        self.count = n_dp * n_rep
        self.index = lax.axis_index("dp") * n_rep + lax.axis_index("rep")
        self.levels = []
        stride, left = 1, self.count
        for size in (2, *[4] * 8):
            while size > 1 and left % size:
                size //= 2
            if size > 1:
                self.levels.append((stride, size))
                stride, left = stride * size, left // size
        assert left == 1

    def place(self, level):
        stride, size = level
        return lax.rem(lax.div(self.index, stride), size)

    def swap(self, value, level, d):
        stride, size = level
        return lax.ppermute(value, AXES, [(i, i + ((i // stride % size ^ d) - i // stride % size) * stride) for i in range(self.count)])

    def scatter_sum(self, value, level, other=None):
        size = level[1]
        value = value.reshape(size, value.shape[0] // size, value.shape[1])
        mine = self.place(level)
        got = [self.swap(lax.dynamic_index_in_dim(value, mine ^ d, 0, keepdims=False), level, d) for d in range(1, size)]
        if other is not None:
            got = after(got, other)
        total = lax.dynamic_index_in_dim(value, mine, 0, keepdims=False).astype(f32)
        for g in got:
            total = total + g.astype(f32)
        return total.astype(bf16)

    def gather(self, value, level, other=None):
        size = level[1]
        mine = self.place(level)
        got = [self.swap(value, level, d) for d in range(1, size)]
        if other is not None:
            got = after(got, other)
        out = jnp.zeros((size, *value.shape), value.dtype)
        for d, g in enumerate([value, *got]):
            out = lax.dynamic_update_index_in_dim(out, g, mine ^ d, 0)
        return out.reshape(size * value.shape[0], value.shape[1])

    def exchange_sum(self, value, level, other):
        terms = [value] + after([self.swap(value, level, d) for d in range(1, level[1])], other)
        terms = [t.astype(f32) for t in terms]
        while len(terms) > 1:
            terms = [a + b for a, b in zip(terms[::2], terms[1::2], strict=True)]
        return terms[0].astype(bf16)

    def pair_sum(self, keep, send):
        got = self.swap(send, self.levels[0], 1)
        rows = keep.shape[0] // 4
        cut = [slice(d * rows, (d + 1) * rows) for d in range(4)]
        return [(keep[c].astype(f32) + got[c].astype(f32)).astype(bf16) for c in cut]

    def quarter_sum(self, quarters, other):
        got = after([self.swap(quarters[d], self.levels[1], d) for d in range(1, 4)], other)
        total = quarters[0].astype(f32)
        for g in got:
            total = total + g.astype(f32)
        return total.astype(bf16)

    def join(self, value):
        return jnp.concatenate([value, self.swap(value, self.levels[0], 1)], axis=0)

    def joint_pieces(self, both):
        quad = self.levels[1]
        return [both] + [self.swap(both, quad, d) for d in range(1, quad[1])]

    def pieces(self, value, other):
        quad = self.levels[1]
        own = [value] + after([self.swap(value, quad, d) for d in range(1, quad[1])], other)
        return own + [self.swap(p, self.levels[0], 1) for p in own]


def after(value, other):
    return lax.optimization_barrier((value, other))[0]


def body(packet_bytes, owner_index, session_id, class_label, byte_table, w_conv, norm_gain, w_project, w_out, w_head):
    groups = lax.axis_size("dp")
    devices = Levels(groups, lax.axis_size("rep"))
    packets, length = packet_bytes.shape
    slots = 2 * packets
    capacity = slots // groups
    width = w_conv.shape[1]
    window = w_conv.shape[0]
    vocab, chan = byte_table.shape
    sessions = class_label.shape[0]
    place = lax.rem(devices.index, 8).reshape(1)

    owner = owner_index.reshape(1, packets)
    table_t = byte_table.T
    outgoing, slope, codes = embed(packet_bytes, owner, session_id.reshape(1, packets), table_t, w_conv, capacity, slots)

    def exchange(rows):
        return lax.all_to_all(
            rows.reshape(groups, capacity, rows.shape[1]), "dp", split_axis=0, concat_axis=0, tiled=True
        ).reshape(rows.shape)

    logits, back, keep, send, gain_grad = session_layer(
        place,
        exchange(outgoing),
        class_label.reshape(1, sessions),
        norm_gain.reshape(1, width),
        w_project,
        w_out,
        w_head,
        sessions,
    )
    early = devices.pair_sum(keep, send)
    used = window * width // (2 * LANES) + chan * vocab // (2 * LANES) + 16
    unit = 64
    half_rows = -(-used // unit) * unit
    _, _, *upper = devices.levels
    keep, send = conv_back(
        place, after(exchange(back), early), owner, codes, slope, table_t, w_conv, gain_grad, capacity, half_rows
    )
    early = devices.quarter_sum(early, keep)
    late = devices.pair_sum(keep, send)
    for level in upper:
        early = devices.scatter_sum(early, level, late)
    late = devices.quarter_sum(late, early)
    for level in upper[::-1]:
        early = devices.gather(early, level)
    for level in upper:
        late = devices.exchange_sum(late, level, early)
    late = devices.join(late)
    grad_project, grad_out, grad_head = assemble(
        early_out_kernel, place, devices.pieces(early, late), [w_project.shape, w_out.shape, w_head.shape], "early_out"
    )
    grad_conv, table_grad, gain_grad = assemble(
        late_out_kernel, after(place, grad_head), devices.joint_pieces(late), [w_conv.shape, table_t.shape, (1, width)], "late_out"
    )
    return (logits, table_grad.T, grad_conv, gain_grad.reshape(width), grad_project, grad_out, grad_head)


def solution(mesh):
    split = P(AXES)
    rows = P(AXES, None)
    in_specs = (rows, split, split, split, P(), P(), P(), P(), P(), P())
    out_specs = (rows, P(), P(), P(), P(), P(), P())
    return jax.shard_map(body, mesh=mesh, in_specs=in_specs, out_specs=out_specs, check_vma=False)
```

```python
import functools

import jax
import jax.numpy as jnp
from jax import lax
from jax.experimental import pallas as pl
from jax.experimental.pallas import tpu as pltpu
from jax.sharding import PartitionSpec as P

KERNEL = 8
HEADS = 8
NORM_EPS = 1e-06
WIN_STEP = 8
BYTE_STEP = 4
LANES = 128
VMEM_LIMIT = 28 * 2**20

f32 = jnp.float32
bf16 = jnp.bfloat16
AXES = ("dp", "rep")


def iota(shape, dim):
    return lax.broadcasted_iota(jnp.int32, shape, dim)


def dot_nn(a, b):
    return jnp.dot(a, b, preferred_element_type=f32)


def dot_nt(a, b):
    return lax.dot_general(a, b, (((1,), (1,)), ((), ())), preferred_element_type=f32)


def dot_tn(a, b):
    return lax.dot_general(a, b, (((0,), (0,)), ((), ())), preferred_element_type=f32)


def two_parts(value):
    high = value.astype(bf16)
    return high, (value - high.astype(f32)).astype(bf16)


def flag(mask):
    return jnp.where(mask, 1.0, 0.0).astype(bf16)


def onehot(codes, values):
    return jnp.where(codes == values, jnp.ones((), bf16), jnp.zeros((), bf16))


def small_iota(shape, dim):
    return iota(shape, dim).astype(f32).astype(bf16)


def spread(row, lanes):
    return jnp.broadcast_to(row.astype(f32), (lanes, row.shape[1])).T


def column(row):
    return spread(row, LANES)[:, 0:1].astype(jnp.int32)


def cost(flops, moved):
    return pl.CostEstimate(flops=int(flops), bytes_accessed=int(moved), transcendentals=0)


def slot_places(owner_ref, slots, capacity):
    own_row = owner_ref[...]
    packets = own_row.shape[1]
    ahead = (column(own_row) == own_row) & (iota((packets, packets), 0) < iota((packets, packets), 1))
    rank = jnp.sum(jnp.where(ahead, 1.0, 0.0), axis=0, keepdims=True).astype(jnp.int32)
    return flag(iota((slots, packets), 0) == own_row * capacity + rank)


def embed_kernel(
    capacity,
    bytes_ref,
    owner_ref,
    sess_ref,
    table_ref,
    w_ref,
    out_ref,
    slope_ref,
    codes_ref,
    emb_ref,
    turned_ref,
    w_turned_ref,
):
    step = pl.program_id(0)
    packets, length = bytes_ref.shape
    positions = length // KERNEL
    chan, vocab = table_ref.shape
    width = w_ref.shape[1]

    @pl.when(step == 0)
    def _():
        emb_ref[...] = jnp.zeros_like(emb_ref)
        w_turned_ref[...] = w_ref[...].astype(f32).T.astype(bf16)
        turned_ref[...] = bytes_ref[...].astype(f32).T
        for j in range(KERNEL):
            codes_ref[j] = turned_ref[pl.ds(j, positions, stride=KERNEL), :].astype(bf16)

    here = WIN_STEP * KERNEL
    codes = turned_ref[pl.ds(pl.multiple_of(step * here, here), here), :].astype(jnp.int32)
    parts = [table_ref[:, at : at + LANES].astype(f32) for at in range(0, vocab, LANES)]
    windows = []
    for w in range(WIN_STEP):
        rows = []
        for j in range(w * KERNEL, (w + 1) * KERNEL):
            code = jnp.broadcast_to(codes[j : j + 1, :], (chan, packets))
            lane = code & (LANES - 1)
            found = [jnp.take_along_axis(p, lane, axis=1, mode="promise_in_bounds") for p in parts]
            rows.append(jnp.where(code < LANES, found[0], found[1]).astype(bf16))
        windows.append(jnp.concatenate(rows, axis=0))
    conv = dot_nn(w_turned_ref[...], jnp.concatenate(windows, axis=1))
    sigma = jax.nn.sigmoid(conv)
    act = conv * sigma
    slope_ref[...] = ((sigma + act * (1.0 - sigma)) * (1.0 / positions)).astype(bf16)
    total = emb_ref[...]
    for w in range(WIN_STEP):
        total += act[:, w * packets : (w + 1) * packets]
    emb_ref[...] = total

    @pl.when(step == pl.num_programs(0) - 1)
    def _():
        emb = (emb_ref[...] * (1.0 / positions)).astype(bf16)
        place = slot_places(owner_ref, out_ref.shape[0], capacity)
        out_ref[:, :width] = dot_nt(place, emb).astype(bf16)
        label = spread(sess_ref[...] + 1, LANES).astype(bf16)
        out_ref[:, width:] = dot_nn(place, label).astype(bf16)


def embed(packet_bytes, owner, session, table_t, w_conv, capacity, slots):
    packets, length = packet_bytes.shape
    rows = WIN_STEP * packets
    steps = length // (KERNEL * WIN_STEP)
    width = w_conv.shape[1]
    whole = lambda a: pl.BlockSpec(a.shape, lambda i: (0, 0))
    args = (packet_bytes, owner, session, table_t, w_conv)
    return pl.pallas_call(
        functools.partial(embed_kernel, capacity),
        grid=(steps,),
        in_specs=[whole(a) for a in args],
        out_specs=[
            pl.BlockSpec((slots, width + LANES), lambda i: (0, 0)),
            pl.BlockSpec((width, rows), lambda i: (0, i)),
            pl.BlockSpec((KERNEL, length // KERNEL, packets), lambda i: (0, 0, 0)),
        ],
        out_shape=[
            jax.ShapeDtypeStruct((slots, width + LANES), bf16),
            jax.ShapeDtypeStruct((width, steps * rows), bf16),
            jax.ShapeDtypeStruct((KERNEL, length // KERNEL, packets), bf16),
        ],
        scratch_shapes=[
            pltpu.VMEM((width, packets), f32),
            pltpu.VMEM((length, packets), f32),
            pltpu.VMEM((width, w_conv.shape[0]), bf16),
        ],
        compiler_params=pltpu.CompilerParams(vmem_limit_bytes=2 * VMEM_LIMIT),
        cost_estimate=cost(1e10, 5e6),
        name="embed",
    )(*args)


def share_out(place_ref, halves_ref, keep_ref, send_ref):
    mine, k = place_ref[0], place_ref[1]
    rows = keep_ref.shape[0] // 4
    for d in range(4):
        at = pl.ds(pl.multiple_of((k ^ d) * rows, 16), rows)
        keep_ref[d * rows : (d + 1) * rows, :] = halves_ref[mine, at, :]
        send_ref[d * rows : (d + 1) * rows, :] = halves_ref[1 - mine, at, :]


def session_kernel(
    core_ref,
    inc_ref,
    label_ref,
    gain_ref,
    wp_ref,
    wo_ref,
    wh_ref,
    logits_ref,
    back_ref,
    keep_ref,
    send_ref,
    gain_grad_ref,
    proj_ref,
    att_ref,
    mix_ref,
    dproj_ref,
    halves_ref,
):
    slots = inc_ref.shape[0]
    width = wo_ref.shape[0]
    classes = wh_ref.shape[1]
    sessions = logits_ref.shape[0]
    head = width // HEADS
    scale = head**-0.5

    embedding = inc_ref[:, :width]
    x = embedding.astype(f32)
    tags = inc_ref[:, width:].astype(f32)
    tag_col = tags[:, 0:1]
    tag_row = tags.T[0:1, :]
    gain = gain_ref[...].astype(f32)
    inverse = lax.rsqrt(jnp.mean(x * x, axis=1, keepdims=True) + NORM_EPS)
    norm_in = (x * inverse * gain).astype(bf16)
    proj_ref[...] = dot_nn(norm_in, wp_ref[...]).astype(bf16)

    def part(ref, which, h):
        at = which * width + h * head
        return ref[:, at : at + head]

    same = tag_col == tag_row
    for h in range(HEADS):
        scores = dot_nt(part(proj_ref, 0, h), part(proj_ref, 1, h)) * scale
        scores = jnp.where(same, scores, -1e30)
        shifted = jnp.exp(scores - jnp.max(scores, axis=1, keepdims=True))
        mixing = shifted / jnp.sum(shifted, axis=1, keepdims=True)
        mix_ref[h] = mixing
        att_ref[:, h * head : (h + 1) * head] = dot_nn(mixing.astype(bf16), part(proj_ref, 2, h)).astype(bf16)

    is_member = tag_row == (iota((sessions, slots), 0) + 1).astype(f32)
    member = flag(is_member)
    member_t = flag(tag_col == (iota((slots, sessions), 1) + 1).astype(f32))
    counts = jnp.maximum(jnp.sum(jnp.where(is_member, 1.0, 0.0), axis=1, keepdims=True), 1.0)
    att_high, att_low = two_parts(dot_nn(member, att_ref[...]))
    out_sum = dot_nn(att_high, wo_ref[...]) + dot_nn(att_low, wo_ref[...])
    pooled_b = ((dot_nn(member, embedding) + out_sum) / counts).astype(bf16)
    logits = dot_nn(pooled_b, wh_ref[...])
    logits_ref[...] = logits
    grown = jnp.exp(logits - jnp.max(logits, axis=1, keepdims=True))
    probs = grown / jnp.sum(grown, axis=1, keepdims=True)
    target = jnp.where(column(label_ref[...])[:sessions] == iota((sessions, classes), 1), 1.0, 0.0)
    dlogits = (probs - target) * (1.0 / sessions)
    dl_high, dl_low = two_parts(dlogits)
    grad_head = dot_tn(pooled_b, dl_high) + dot_tn(pooled_b, dl_low)
    dpooled = dot_nt(dl_high, wh_ref[...]) + dot_nt(dl_low, wh_ref[...])
    dsess = dpooled / counts
    dsess_b, dsess_low = two_parts(dsess)
    dhidden = dot_nn(member_t, dsess_b) + dot_nn(member_t, dsess_low)
    grad_out = dot_tn(att_high, dsess_b) + dot_tn(att_low, dsess_b)
    datt_s = dot_nt(dsess_b, wo_ref[...]).astype(bf16)
    datt = dot_nn(member_t, datt_s).astype(bf16)

    for h in range(HEADS):
        cols = slice(h * head, (h + 1) * head)
        mixing = mix_ref[h]
        dmix_s = dot_nt(datt_s[:, cols], part(proj_ref, 2, h))
        dmixing = jnp.sum(jnp.where(is_member, dmix_s, 0.0), axis=0, keepdims=True)
        weighted = mixing * dmixing
        dscores = ((weighted - mixing * jnp.sum(weighted, axis=1, keepdims=True)) * scale).astype(bf16)
        dq = dot_nn(dscores, part(proj_ref, 1, h))
        dk = dot_tn(dscores, part(proj_ref, 0, h))
        dv = dot_tn(mixing.astype(bf16), datt[:, cols])
        for which, d in ((0, dq), (1, dk), (2, dv)):
            at = which * width + h * head
            dproj_ref[:, at : at + head] = d.astype(bf16)

    at = [0, 0]

    def put(half, block):
        for s in range(block.shape[1] // LANES):
            rows = block.shape[0]
            halves_ref[half, at[half] : at[half] + rows, :] = block[:, s * LANES : (s + 1) * LANES].astype(bf16)
            at[half] += rows

    side = 3 * width // 2
    for half in range(2):
        put(half, dot_tn(norm_in, dproj_ref[:, half * side : (half + 1) * side]))
        put(half, grad_out[:, half * width // 2 : (half + 1) * width // 2])
        put(half, grad_head[half * width // 2 : (half + 1) * width // 2, :])
    share_out(core_ref, halves_ref, keep_ref, send_ref)
    dnorm = dot_nt(dproj_ref[...], wp_ref[...])
    grad_gain = jnp.sum(dnorm * x * inverse, axis=0, keepdims=True)
    gain_grad_ref[...] = jnp.zeros_like(gain_grad_ref)
    for s in range(width // LANES):
        gain_grad_ref[s : s + 1, :] = grad_gain[:, s * LANES : (s + 1) * LANES]
    scaled = dnorm * gain
    slant = jnp.mean(x * scaled, axis=1, keepdims=True) * (inverse * inverse * inverse)
    back_ref[...] = (inverse * scaled - x * slant + dhidden).astype(bf16)


def session_layer(core, incoming, labels, gain, w_project, w_out, w_head, sessions):
    slots = incoming.shape[0]
    width = w_out.shape[0]
    classes = w_head.shape[1]
    half_rows = width * (3 * width + width + classes) // (2 * LANES)
    args = (core, incoming, labels, gain, w_project, w_out, w_head)
    vmem = pl.BlockSpec(memory_space=pltpu.VMEM)
    half = jax.ShapeDtypeStruct((half_rows, LANES), bf16)
    return pl.pallas_call(
        session_kernel,
        in_specs=[pl.BlockSpec(memory_space=pltpu.SMEM)] + [vmem] * (len(args) - 1),
        out_specs=[vmem] * 5,
        out_shape=[
            jax.ShapeDtypeStruct((sessions, classes), f32),
            jax.ShapeDtypeStruct((slots, width), bf16),
            half,
            half,
            jax.ShapeDtypeStruct((16, LANES), f32),
        ],
        scratch_shapes=[
            pltpu.VMEM((slots, 3 * width), bf16),
            pltpu.VMEM((slots, width), bf16),
            pltpu.VMEM((HEADS, slots, slots), f32),
            pltpu.VMEM((slots, 3 * width), bf16),
            pltpu.VMEM((2, half_rows, LANES), bf16),
        ],
        compiler_params=pltpu.CompilerParams(vmem_limit_bytes=VMEM_LIMIT),
        cost_estimate=cost(1e10, 5e6),
        name="session_layer",
    )(*args)


def add_by_value(codes_ref, dconv_ref, table_ref, w_ref, rows_ref, table_grad_ref, step):
    places, positions, packets = codes_ref.shape
    chan, vocab = table_ref.shape
    values = small_iota((vocab, packets), 0)
    blocks = []
    for i in range(places):
        codes = codes_ref[i]
        blocks.append(jnp.concatenate([onehot(codes[w : w + 1, :], values) for w in range(positions)], axis=1))
    sums = dot_nn(jnp.concatenate(blocks, axis=0), dconv_ref[...]).astype(bf16)
    for i in range(places):
        by_value = sums[i * vocab : (i + 1) * vocab]
        at = pl.ds(pl.multiple_of((step * places + i) * chan, chan), chan)
        table_grad_ref[...] += dot_nt(w_ref[at, :], by_value)
        rows_ref[at, :] = dot_nn(table_ref[...], by_value).astype(bf16)


def conv_back_kernel(
    capacity,
    core_ref,
    ret_ref,
    owner_ref,
    codes_ref,
    slope_ref,
    table_ref,
    w_ref,
    gain_grad_ref,
    keep_ref,
    send_ref,
    dconv_ref,
    rows_ref,
    table_grad_ref,
    halves_ref,
):
    j = pl.program_id(0)
    slots, width = ret_ref.shape
    packets = owner_ref.shape[1]
    chan, vocab = table_ref.shape
    window = w_ref.shape[0]

    @pl.when(j == 0)
    def _():
        demb = dot_tn(slot_places(owner_ref, slots, capacity), ret_ref[...])
        halves_ref[...] = jnp.zeros_like(halves_ref)
        table_grad_ref[...] = jnp.zeros_like(table_grad_ref)
        for first in range(0, slope_ref.shape[1], packets):
            at = slice(first, first + packets)
            dconv_ref[at, :] = (demb * slope_ref[:, at].astype(f32).T).astype(bf16)

    add_by_value(codes_ref, dconv_ref, table_ref, w_ref, rows_ref, table_grad_ref, j)

    @pl.when(j == pl.num_programs(0) - 1)
    def _():
        wide = width // (2 * LANES)
        for half in range(2):
            for s in range(wide):
                slab = half * wide + s
                halves_ref[half, s * window : (s + 1) * window, :] = rows_ref[:, slab * LANES : (slab + 1) * LANES]
            end = wide * window
            table_part = table_grad_ref[:, half * vocab // 2 : (half + 1) * vocab // 2]
            halves_ref[half, end : end + chan, :] = table_part.astype(bf16)
        halves_ref[0, end + chan : end + chan + 16, :] = gain_grad_ref[...].astype(bf16)
        share_out(core_ref, halves_ref, keep_ref, send_ref)


def whole(a):
    return pl.BlockSpec(a.shape, lambda j: (0,) * len(a.shape))


def conv_back(core, returned, owner, codes, slope, table_t, w_conv, gain_grad, capacity, half_rows):
    args = (returned, owner, codes, slope, table_t, w_conv, gain_grad)
    specs = [whole(a) if a.ndim == 2 else pl.BlockSpec((BYTE_STEP, *a.shape[1:]), lambda j: (j, 0, 0)) for a in args]
    half = jax.ShapeDtypeStruct((half_rows, LANES), bf16)
    return pl.pallas_call(
        functools.partial(conv_back_kernel, capacity),
        grid=(KERNEL // BYTE_STEP,),
        in_specs=[pl.BlockSpec(memory_space=pltpu.SMEM), *specs],
        out_specs=[whole(half), whole(half)],
        out_shape=[half, half],
        scratch_shapes=[
            pltpu.VMEM(slope.shape[::-1], bf16),
            pltpu.VMEM(w_conv.shape, bf16),
            pltpu.VMEM(table_t.shape, f32),
            pltpu.VMEM((2, half_rows, LANES), bf16),
        ],
        compiler_params=pltpu.CompilerParams(vmem_limit_bytes=28 * 2**20),
        cost_estimate=cost(1e9, 1e6),
        name="conv_back",
    )(core, *args)


def put_together(place_ref, piece_refs, halves_ref):
    mine, k = place_ref[0], place_ref[1]
    count = 4
    rows = halves_ref.shape[1] // count
    for d in range(count):
        at = pl.multiple_of((k ^ d) * rows, 16)
        if len(piece_refs) == count:
            own, other = piece_refs[d][0:rows, :], piece_refs[d][rows : 2 * rows, :]
        else:
            own, other = piece_refs[d][...], piece_refs[count + d][...]
        halves_ref[mine, pl.ds(at, rows), :] = own
        halves_ref[1 - mine, pl.ds(at, rows), :] = other


def early_out_kernel(place_ref, *refs):
    *pieces, project_ref, out_ref, head_ref, halves_ref = refs
    put_together(place_ref, pieces, halves_ref)
    for half in range(2):
        at = 0
        for ref in (project_ref, out_ref):
            rows, side = ref.shape[0], ref.shape[1] // 2
            for s in range(side // LANES):
                lanes = half * side + s * LANES
                ref[:, lanes : lanes + LANES] = halves_ref[half, at : at + rows, :].astype(f32)
                at += rows
        rows = head_ref.shape[0] // 2
        head_ref[half * rows : (half + 1) * rows, :] = halves_ref[half, at : at + rows, :].astype(f32)


def late_out_kernel(place_ref, *refs):
    *pieces, conv_ref, table_ref, gain_ref, halves_ref = refs
    put_together(place_ref, pieces, halves_ref)
    for half in range(2):
        at = 0
        rows, side = conv_ref.shape[0], conv_ref.shape[1] // 2
        for s in range(side // LANES):
            lanes = half * side + s * LANES
            conv_ref[:, lanes : lanes + LANES] = halves_ref[half, at : at + rows, :].astype(f32)
            at += rows
        chan, vocab = table_ref.shape
        table_ref[:, half * vocab // 2 : (half + 1) * vocab // 2] = halves_ref[half, at : at + chan, :].astype(f32)
        at += chan
        if half == 0:
            gain = halves_ref[0, at : at + 16, :].astype(f32)
            for s in range(gain_ref.shape[1] // LANES):
                gain_ref[:, s * LANES : (s + 1) * LANES] = gain[s : s + 1, :]


def assemble(kernel, place, pieces, shapes, name):
    vmem = pl.BlockSpec(memory_space=pltpu.VMEM)
    rows = sum(p.shape[0] for p in pieces) // 2
    return pl.pallas_call(
        kernel,
        in_specs=[pl.BlockSpec(memory_space=pltpu.SMEM)] + [vmem] * len(pieces),
        out_specs=[vmem] * len(shapes),
        out_shape=[jax.ShapeDtypeStruct(s, f32) for s in shapes],
        scratch_shapes=[pltpu.VMEM((2, rows, LANES), bf16)],
        compiler_params=pltpu.CompilerParams(vmem_limit_bytes=VMEM_LIMIT),
        cost_estimate=cost(1e9, 5e6),
        name=name,
    )(place, *pieces)


class Levels:
    def __init__(self, n_dp, n_rep):
        self.count = n_dp * n_rep
        self.index = lax.axis_index("dp") * n_rep + lax.axis_index("rep")
        self.levels = []
        stride, left = 1, self.count
        for size in (2, *[4] * 8):
            while size > 1 and left % size:
                size //= 2
            if size > 1:
                self.levels.append((stride, size))
                stride, left = stride * size, left // size
        assert left == 1

    def place(self, level):
        stride, size = level
        return lax.rem(lax.div(self.index, stride), size)

    def swap(self, value, level, d):
        stride, size = level
        return lax.ppermute(value, AXES, [(i, i + ((i // stride % size ^ d) - i // stride % size) * stride) for i in range(self.count)])

    def scatter_sum(self, value, level, other=None):
        size = level[1]
        value = value.reshape(size, value.shape[0] // size, value.shape[1])
        mine = self.place(level)
        got = [self.swap(lax.dynamic_index_in_dim(value, mine ^ d, 0, keepdims=False), level, d) for d in range(1, size)]
        if other is not None:
            got = after(got, other)
        total = lax.dynamic_index_in_dim(value, mine, 0, keepdims=False).astype(f32)
        for g in got:
            total = total + g.astype(f32)
        return total.astype(bf16)

    def gather(self, value, level, other=None):
        size = level[1]
        mine = self.place(level)
        got = [self.swap(value, level, d) for d in range(1, size)]
        if other is not None:
            got = after(got, other)
        out = jnp.zeros((size, *value.shape), value.dtype)
        for d, g in enumerate([value, *got]):
            out = lax.dynamic_update_index_in_dim(out, g, mine ^ d, 0)
        return out.reshape(size * value.shape[0], value.shape[1])

    def exchange_sum(self, value, level, other):
        terms = [value] + after([self.swap(value, level, d) for d in range(1, level[1])], other)
        terms = [t.astype(f32) for t in terms]
        while len(terms) > 1:
            terms = [a + b for a, b in zip(terms[::2], terms[1::2], strict=True)]
        return terms[0].astype(bf16)

    def pair_sum(self, keep, send):
        got = self.swap(send, self.levels[0], 1)
        rows = keep.shape[0] // 4
        cut = [slice(d * rows, (d + 1) * rows) for d in range(4)]
        return [(keep[c].astype(f32) + got[c].astype(f32)).astype(bf16) for c in cut]

    def quarter_sum(self, quarters, other):
        got = after([self.swap(quarters[d], self.levels[1], d) for d in range(1, 4)], other)
        total = quarters[0].astype(f32)
        for g in got:
            total = total + g.astype(f32)
        return total.astype(bf16)

    def join(self, value):
        return jnp.concatenate([value, self.swap(value, self.levels[0], 1)], axis=0)

    def joint_pieces(self, both):
        quad = self.levels[1]
        return [both] + [self.swap(both, quad, d) for d in range(1, quad[1])]

    def pieces(self, value, other):
        quad = self.levels[1]
        own = [value] + after([self.swap(value, quad, d) for d in range(1, quad[1])], other)
        return own + [self.swap(p, self.levels[0], 1) for p in own]


def after(value, other):
    return lax.optimization_barrier((value, other))[0]


def body(packet_bytes, owner_index, session_id, class_label, byte_table, w_conv, norm_gain, w_project, w_out, w_head):
    groups = lax.axis_size("dp")
    devices = Levels(groups, lax.axis_size("rep"))
    packets, length = packet_bytes.shape
    slots = 2 * packets
    capacity = slots // groups
    width = w_conv.shape[1]
    window = w_conv.shape[0]
    vocab, chan = byte_table.shape
    sessions = class_label.shape[0]
    place = jnp.stack([devices.place(level) for level in devices.levels[:2]])

    owner = owner_index.reshape(1, packets)
    table_t = byte_table.T
    outgoing, slope, codes = embed(packet_bytes, owner, session_id.reshape(1, packets), table_t, w_conv, capacity, slots)

    def exchange(rows):
        return lax.all_to_all(
            rows.reshape(groups, capacity, rows.shape[1]), "dp", split_axis=0, concat_axis=0, tiled=True
        ).reshape(rows.shape)

    logits, back, keep, send, gain_grad = session_layer(
        place,
        exchange(outgoing),
        class_label.reshape(1, sessions),
        norm_gain.reshape(1, width),
        w_project,
        w_out,
        w_head,
        sessions,
    )
    early = devices.pair_sum(keep, send)
    used = window * width // (2 * LANES) + chan * vocab // (2 * LANES) + 16
    unit = 64
    half_rows = -(-used // unit) * unit
    _, _, *upper = devices.levels
    keep, send = conv_back(
        place, after(exchange(back), early), owner, codes, slope, table_t, w_conv, gain_grad, capacity, half_rows
    )
    early = devices.quarter_sum(early, keep)
    late = devices.pair_sum(keep, send)
    for level in upper:
        early = devices.scatter_sum(early, level, late)
    late = devices.quarter_sum(late, early)
    for level in upper[::-1]:
        early = devices.gather(early, level)
    for level in upper:
        late = devices.exchange_sum(late, level, early)
    late = devices.join(late)
    grad_project, grad_out, grad_head = assemble(
        early_out_kernel, place, devices.pieces(early, late), [w_project.shape, w_out.shape, w_head.shape], "early_out"
    )
    grad_conv, table_grad, gain_grad = assemble(
        late_out_kernel, after(place, grad_head), devices.joint_pieces(late), [w_conv.shape, table_t.shape, (1, width)], "late_out"
    )
    return (logits, table_grad.T, grad_conv, gain_grad.reshape(width), grad_project, grad_out, grad_head)


def solution(mesh):
    split = P(AXES)
    rows = P(AXES, None)
    in_specs = (rows, split, split, split, P(), P(), P(), P(), P(), P())
    out_specs = (rows, P(), P(), P(), P(), P(), P())
    return jax.shard_map(body, mesh=mesh, in_specs=in_specs, out_specs=out_specs, check_vma=False)
```
